32 devices in a mesh: band: 4 (over y, x), patch: 8 (over z, core).
Axes of the slice: x: 2, y: 2, z: 4, core: 2. Of those that a mesh axis runs over, the one named last changes fastest.
Arguments:
- emissivity: float32 [32, 65536], P('band', 'patch'), may hold values from 0.1 to 0.9
- blackbody: float32 [32, 65536], P('band', 'patch'), may hold values from 0.2 to 2
- loss_weights: float32 [32, 65536], P('band', 'patch'), may hold values from 0.5 to 1.5
- view_blocks: bfloat16 [8, 4, 8, 16, 256, 256], P('patch', 'band'), may hold values from 0 to 0.012207031
- column_blocks: int32 [8, 4, 8, 16], P('patch', 'band'), may hold values from 0 to 255, as said below
- patch_owner: int32 [8, 4, 2048, 1], P('patch', 'band'), may hold values from 0 to 31; in each aligned block of 2048 rows (0 to 2047, 2048 to 4095, ..., all dimensions but the last counted through in order) at most 192 rows name the same one
- patch_surface: int32 [8, 4, 2048], P('patch', 'band'), may hold values from 0 to 1023
Outputs:
- radiosity: float32 [32, 8, 4, 2048], P(None, 'patch', 'band')
- surface_grad: float32 [32, 32768], P(None, ('band', 'patch'))
The draws below stay inside these ranges and needn't reach their ends.
Inputs may be any that keep to these rules, and one draw needn't show every extreme that they name: column_blocks[g, s, r] lists 16 different row-block indices, all among the 96 row blocks of patch groups g - 1, g and g + 1, wrapping around the 8 groups. `patch_owner`: among the 2048 patches of one row-block range no owner is named more than 192 times.
All inputs are finite; a program needn't handle non-finite values.
Results may differ from the reference program's by a relative error of at most 0.0005.
Values may be sent and summed in bfloat16 or wider, within the bound.
No kernel may reach another device: no remote copies, remote signals or barrier semaphores. Data moves between devices by JAX's collectives and lax.ppermute only.
A program may use at most 128 MiB of HBM per device.

```python
import math
import jax
import jax.numpy as jnp
import numpy as np
from jax import lax

BANDS = 32
BLK = 256
K = 16
RB_DEV = 8
GROUPS = 8
SPLIT = 4
PD = 2048
PATCHES = 65536
CAP = 192
SURF_DEV = 1024
SURFACES = 32768
DEVICES = 32


def draw_view_blocks(key, part):
    shape = (GROUPS, SPLIT, RB_DEV, K, BLK, BLK)
    mask_key = jax.random.fold_in(key, 11)
    value_key = jax.random.fold_in(key, 23)
    present = (jax.random.randint(mask_key, shape, 0, 8) == 0).astype(jnp.float32)
    unit = jax.random.uniform(value_key, shape, jnp.float32, 0.0, 1.0)
    spread = jnp.exp((unit - 1.0) * jnp.log(100.0))
    top = 33.5
    values = present * spread * (top / (K * BLK))
    return values.astype(jnp.bfloat16)


def draw_column_blocks(key, part):
    per_group = SPLIT * RB_DEV
    row_total = GROUPS * per_group
    keys = jax.random.split(key, row_total)
    picks = jax.vmap(lambda single: jax.random.permutation(single, 3 * per_group)[:K])(keys)
    group_index = jnp.arange(row_total, dtype=jnp.int32) // per_group
    window_start = (group_index - 1) * per_group
    chosen = jnp.mod(window_start[:, None] + picks.astype(jnp.int32), row_total)
    return chosen.reshape(GROUPS, SPLIT, RB_DEV, K).astype(jnp.int32)


def place_ends(array, own_key, smallest, high):
    longest = array.shape.index(max(array.shape))
    spots = []
    for shift in (0, 1):
        where = [jax.random.randint(jax.random.fold_in(own_key, axis), (), 0, length) for axis, length in enumerate(array.shape)]
        where[longest] = (where[longest] + shift) % array.shape[longest]
        spots.append(tuple(where))
    return array.at[spots[0]].set(smallest).at[spots[1]].set(high)


def level_of(stream_key, extent, shards, smallest, top_value):
    def one(dim, shards_of):
        heights = jax.random.uniform(jax.random.fold_in(jax.random.fold_in(stream_key, 6), dim), (shards_of,), jnp.float32, smallest / len(shards), top_value / len(shards))
        return jnp.repeat(jnp.exp(heights), extent[dim] // shards_of).reshape((-1,) + (1,) * (len(extent) - dim - 1))

    gain = one(*shards[0])
    for cut in shards[1:]:
        gain = gain * one(*cut)
    return gain


def assign_block(rng, own, number, rows, count, top, limit, slope):
    sequence = jax.random.permutation(rng, count)
    packed, ordinary = portions_of(count, rows * top, limit, slope, True), portions_of(count, rows * top, limit, slope, False)
    places = jnp.arange(count)

    def named(sizes, offset_by):
        used = int((sizes > 0).sum())
        fixed = max(1, used // 4)
        shifted = fixed + (places - fixed + offset_by * (used - fixed)) % max(1, count - fixed)
        return jnp.zeros((count,), jnp.int32).at[sequence[jnp.where(places < fixed, places, shifted)]].set(jnp.asarray(sizes, jnp.int32))

    sizes = jnp.where(number % 4 == 0, named(packed, number // 4), named(ordinary, number - number // 4 - 1))
    mixed = jax.random.permutation(jax.random.fold_in(own, 3), count)
    donor, taker = mixed[0:count // 2 * 2:2], mixed[1:count // 2 * 2:2]
    room = jnp.minimum(sizes[donor] - 1, limit - sizes[taker]) // 2
    room = jnp.where((donor == sequence[0]) | (taker == sequence[0]) | (sizes[taker] == 0), 0, jnp.maximum(room, 0))
    shifted = jax.random.randint(jax.random.fold_in(own, 4), (count // 2,), 0, 1 << 20) % (room + 1)
    sizes = sizes.at[donor].add(-shifted).at[taker].add(shifted)
    labels = jnp.searchsorted(jnp.cumsum(sizes), jnp.arange(rows * top), side="right").astype(jnp.int32)
    table = labels.reshape(top, rows).T
    table = table[jax.random.permutation(jax.random.fold_in(own, 1), rows)]
    offset_by = jax.random.randint(jax.random.fold_in(own, 2), (rows, 1), 0, top)
    return jnp.take_along_axis(table, (jnp.arange(top)[None, :] + offset_by) % top, axis=1)


def portions_of(number_of, total, limit, slope, full):
    portions = [(1 << 20) // math.isqrt(standing ** slope) + 1 for standing in range(1, number_of + 1)]
    largest = limit if full else min(limit, max(-(-total // number_of), total * portions[0] // sum(portions)))
    least = 1 if total - largest >= number_of - 1 else 0
    holding, rest = [largest] + [least] * (number_of - 1), total - largest - least * (number_of - 1)
    while rest > 0:
        candidates = [i for i in range(1, number_of) if holding[i] < largest] or [i for i in range(1, number_of) if holding[i] < limit]
        pool, budget = sum([portions[i] for i in candidates]), rest
        for i in candidates:
            extra = min(limit - holding[i], max(1, budget * portions[i] // pool), rest)
            holding[i] = holding[i] + extra
            rest = rest - extra
    return np.array(holding)


def setup_inputs(seed: int = 0) -> dict:
    streams_of = jax.random.split(jax.random.key(seed), 8)
    emissivity = jnp.clip(0.1 + 0.79999997 * jax.random.uniform(streams_of[0], (BANDS, PATCHES), jnp.float32) ** level_of(streams_of[0], (BANDS, PATCHES), ((0, 4), (1, 8)), -0.2, 0.2), 0.1, 0.9)
    blackbody = jnp.clip(jnp.exp(math.log(2.0) - 2.3025851 * jax.random.uniform(streams_of[1], (BANDS, PATCHES), jnp.float32) ** level_of(streams_of[1], (BANDS, PATCHES), ((0, 4), (1, 8)), -0.2, 0.2)), 0.2, 2.0)
    loss_weights = jnp.clip(0.5 + 1.0 * jax.random.uniform(streams_of[2], (BANDS, PATCHES), jnp.float32) ** level_of(streams_of[2], (BANDS, PATCHES), ((0, 4), (1, 8)), -0.2, 0.2), 0.5, 1.5)
    view_blocks = draw_view_blocks(jax.random.fold_in(streams_of[7], 71), 0)
    column_blocks = draw_column_blocks(jax.random.fold_in(streams_of[7], 71), 0)
    patch_owner_keys = jax.random.split(jax.random.fold_in(streams_of[5], 1), GROUPS * SPLIT * PD // PD)
    patch_owner_turns = jax.random.permutation(jax.random.fold_in(streams_of[5], 3), GROUPS * SPLIT * PD // PD)
    patch_owner = jax.vmap(lambda own, number: assign_block(jax.random.fold_in(streams_of[5], 2), own, number, PD, DEVICES, 1, CAP, 2))(patch_owner_keys, patch_owner_turns).reshape((GROUPS, SPLIT, PD, 1))
    patch_surface = place_ends(jax.random.randint(streams_of[6], (GROUPS, SPLIT, PD), 0, SURF_DEV), jax.random.fold_in(streams_of[6], 1), 0, SURF_DEV - 1).astype(jnp.int32)
    return {"emissivity": emissivity, "blackbody": blackbody, "loss_weights": loss_weights, "view_blocks": view_blocks, "column_blocks": column_blocks, "patch_owner": patch_owner, "patch_surface": patch_surface}


def reference(emissivity, blackbody, loss_weights, view_blocks, column_blocks, patch_owner, patch_surface):
    block_total = GROUPS * SPLIT * RB_DEV
    emission = emissivity * blackbody
    reflect = 1.0 - emissivity
    matrix = view_blocks.reshape(block_total, K, BLK, BLK)
    columns = column_blocks.reshape(block_total, K).astype(jnp.int32)

    def forward(vector):
        blocks = vector.reshape(BANDS, block_total, BLK)

        def row_block(element):
            values, where = element
            picked = jnp.take(blocks, where, axis=1).astype(jnp.float32)
            return jnp.einsum('kij,bkj->bi', values.astype(jnp.float32), picked)

        result = lax.map(row_block, (matrix, columns))
        return jnp.transpose(result, (1, 0, 2)).reshape(BANDS, PATCHES)

    def adjoint(vector):
        blocks = jnp.transpose(vector.reshape(BANDS, block_total, BLK), (1, 0, 2))

        def accumulate(total, element):
            values, where, source = element
            partial_terms = jnp.einsum('kij,bi->bkj', values.astype(jnp.float32), source.astype(jnp.float32))
            return total.at[:, where].add(partial_terms), None

        start = jnp.zeros((BANDS, block_total, BLK), jnp.float32)
        total, unused = lax.scan(accumulate, start, (matrix, columns, blocks))
        return total.reshape(BANDS, PATCHES)

    incident_zero = forward(emission.astype(jnp.bfloat16))
    rad_one = emission + reflect * incident_zero
    incident_one = forward(rad_one.astype(jnp.bfloat16))
    radiosity = emission + reflect * incident_one
    adjoint_one = adjoint((reflect * loss_weights).astype(jnp.bfloat16))
    adjoint_zero = adjoint((reflect * adjoint_one).astype(jnp.bfloat16))
    gradient = (loss_weights + adjoint_one + adjoint_zero) * blackbody - (loss_weights * incident_one + adjoint_one * incident_zero)
    surface_ids = (patch_owner.reshape(PATCHES) * SURF_DEV + patch_surface.reshape(PATCHES)).astype(jnp.int32)
    surface_sums = jax.ops.segment_sum(gradient.T, surface_ids, SURFACES)
    surface_counts = jax.ops.segment_sum(jnp.ones((PATCHES,), jnp.float32), surface_ids, SURFACES)
    surface_grad = (surface_sums / jnp.maximum(surface_counts, 1.0)[:, None]).T
    return radiosity.reshape(BANDS, GROUPS, SPLIT, PD), surface_grad
```

```python
import jax
import jax.numpy as jnp
from jax import lax
from jax.experimental import pallas as pl
from jax.experimental.pallas import tpu as pltpu
from jax.sharding import PartitionSpec as P

F32 = jnp.float32
BF16 = jnp.bfloat16
LANES = 128
MIB = 1 << 20
VMEM = pl.BlockSpec(memory_space=pltpu.VMEM)
SMEM = pl.BlockSpec(memory_space=pltpu.SMEM)


def local_kernel(kernel, outs, ins, scratch=(), limit=24 * MIB, flops=0, touched=0):
    return pl.pallas_call(
        kernel,
        out_shape=outs,
        in_specs=ins,
        out_specs=jax.tree.map(lambda _: VMEM, outs),
        scratch_shapes=scratch,
        compiler_params=pltpu.CompilerParams(vmem_limit_bytes=limit),
        cost_estimate=pl.CostEstimate(flops=flops, bytes_accessed=touched, transcendentals=0),
    )


def shape(dims, dtype):
    return jax.ShapeDtypeStruct(dims, dtype)


def nt(a, b):
    return lax.dot_general(a, b, (((1,), (1,)), ((), ())), preferred_element_type=F32)


def nn(a, b):
    return lax.dot_general(a, b, (((1,), (0,)), ((), ())), preferred_element_type=F32)


def body(
    emissivity, blackbody, loss_weights, view_blocks, column_blocks, patch_owner, patch_surface
):
    split = lax.axis_size("band")
    groups = lax.axis_size("patch")
    devices = split * groups
    part_bands = emissivity.shape[0]
    bands = part_bands * split
    rb_count, depth, width = view_blocks.shape[2:5]
    rows = rb_count * width
    per_group = split * rb_count
    capacity = max(2, 3 * rows // devices)
    surfaces = rows // 2
    pack = LANES // bands
    share = capacity // pack
    me = lax.axis_index("patch")

    def inner(block):
        return lax.ppermute(block, "patch", [(i, i ^ 1) for i in range(groups)])

    def outer(block):
        return lax.ppermute(
            block, "patch", [(i, (i + (1 if i % 2 else -1)) % groups) for i in range(groups)]
        )

    def exchange(block):
        return lax.all_to_all(block, "band", 0, 0)

    columns = column_blocks.reshape(rb_count * depth)
    column_group = columns // per_group
    third = jnp.where(column_group == me, 0, jnp.where(column_group == (me ^ 1), 1, 2))
    slots = third * per_group + columns % per_group
    matrix = view_blocks.reshape(rb_count, depth, width, width)
    block_shape = (rb_count, bands, width)
    gathered_shape = (split, rb_count, bands, width)
    pass_flops = 2 * bands * rb_count * depth * width * width

    def prepare(e_ref, b_ref, w_ref, small_ref, full_ref):
        for c in range(per_group):
            cut = slice(c * width, (c + 1) * width)
            owner, r = c // rb_count, c % rb_count
            e, b, w = e_ref[:, cut], b_ref[:, cut], w_ref[:, cut]
            start = (e * b).astype(BF16)
            for d in range(split):
                small_ref[d, c] = start
            small_ref[owner, per_group + r] = ((1.0 - e) * w).astype(BF16)
            full_ref[owner, 0, r] = e
            full_ref[owner, 1, r] = b
            full_ref[owner, 2, r] = w

    small, full = local_kernel(
        prepare,
        (
            shape((split, per_group + rb_count, part_bands, width), BF16),
            shape((split, 3, rb_count, part_bands, width), F32),
        ),
        [VMEM] * 3,
    )(emissivity, blackbody, loss_weights)
    small = exchange(small)
    full = exchange(full)

    def of(ref, which, r):
        return jnp.concatenate([ref[s, which, r] for s in range(split)], axis=0)

    def scatter_products(slots_ref, m_ref, own_ref, in_ref, out_ref, held, total):
        total[...] = jnp.zeros_like(total)

        def step(i, carry):
            for q in range(2):
                r = i * 2 + q
                u = held[r]
                for k in range(depth):
                    s = slots_ref[r * depth + k]
                    total[s] += nn(u, m_ref[r, k])
            return carry

        lax.fori_loop(0, rb_count // 2, step, 0)
        for s in range(split):
            at = s * rb_count
            own_ref[s] = total[at : at + rb_count]
            in_ref[s] = total[per_group + at : per_group + at + rb_count].astype(BF16)
            out_ref[s] = total[2 * per_group + at : 2 * per_group + at + rb_count].astype(BF16)

    part_outs = (shape(gathered_shape, F32), shape(gathered_shape, BF16), shape(gathered_shape, BF16))
    part_scratch = [pltpu.VMEM(block_shape, BF16), pltpu.VMEM((3 * per_group, bands, width), F32)]

    def adjoint_first(slots_ref, m_ref, small_ref, own_ref, in_ref, out_ref, held, total):
        for r in range(rb_count):
            u = [small_ref[s, per_group + r].astype(F32) for s in range(split)]
            held[r] = jnp.concatenate(u, axis=0).astype(BF16)
        scatter_products(slots_ref, m_ref, own_ref, in_ref, out_ref, held, total)

    def arrived(got_ref, far_ref, r):
        value = far_ref[r]
        for s in range(split):
            value = value + got_ref[s, r].astype(F32)
        return value

    def adjoint_second(
        slots_ref, m_ref, got_ref, far_ref, full_ref, one_ref, own_ref, in_ref, out_ref, held, total
    ):
        for r in range(rb_count):
            value = arrived(got_ref, far_ref, r)
            one_ref[r] = value
            held[r] = ((1.0 - of(full_ref, 0, r)) * value).astype(BF16)
        scatter_products(slots_ref, m_ref, own_ref, in_ref, out_ref, held, total)

    def collect(own, near, far):
        far = exchange(far)
        near = inner(near)
        far = outer(jnp.sum(far.astype(F32), axis=0))
        return exchange((own + near.astype(F32)).astype(BF16)), far

    def products(slots_ref, m_ref, held, finish):
        def step(i, carry):
            for q in range(2):
                r = i * 2 + q
                value = jnp.zeros((bands, width), F32)
                for k in range(depth):
                    value = value + nt(held[slots_ref[r * depth + k]], m_ref[r, k])
                finish(r, value)
            return carry

        lax.fori_loop(0, rb_count // 2, step, 0)

    def forward_first(slots_ref, m_ref, own_ref, in_ref, out_ref, full_ref, zero_ref, rad_ref, held):
        for third_index, ref in enumerate((own_ref, in_ref, out_ref)):

            def fill(c, carry, third_index=third_index, ref=ref):
                pieces = [ref[s, c].astype(F32) for s in range(split)]
                held[third_index * per_group + c] = jnp.concatenate(pieces, axis=0).astype(BF16)
                return carry

            lax.fori_loop(0, per_group, fill, 0)

        def finish(r, value):
            e, b = of(full_ref, 0, r), of(full_ref, 1, r)
            zero_ref[r] = value
            rad = (e * b + (1.0 - e) * value).astype(BF16)
            for d in range(split):
                rad_ref[d, r] = rad

        products(slots_ref, m_ref, held, finish)

    def forward_second(slots_ref, m_ref, own_ref, in_ref, out_ref, full_ref, one_ref, rad_ref, held):
        for third_index, ref in enumerate((own_ref, in_ref, out_ref)):
            for s in range(split):
                at = third_index * per_group + s * rb_count
                held[at : at + rb_count] = ref[s]

        def finish(r, value):
            e, b = of(full_ref, 0, r), of(full_ref, 1, r)
            one_ref[r] = value
            cut = pl.ds(pl.multiple_of(r * width, width), width)
            rad_ref[:, cut] = e * b + (1.0 - e) * value

        products(slots_ref, m_ref, held, finish)

    window_scratch = [pltpu.VMEM((3 * per_group, bands, width), BF16)]

    def route(owner_ref, surface_ref, place_ref, first_ref, label_ref):
        names = lax.broadcasted_iota(jnp.int32, (devices, width), 0)
        upper = (
            lax.broadcasted_iota(jnp.int32, (width, width), 0)
            <= lax.broadcasted_iota(jnp.int32, (width, width), 1)
        ).astype(BF16)
        hits, ranks = [], []
        count = jnp.zeros((devices, 1), F32)
        for c in range(rb_count):
            hit = (owner_ref[:, c * width : (c + 1) * width] == names).astype(F32)
            rank = nn(hit.astype(BF16), upper) + count
            count = rank[:, width - 1 : width]
            hits.append(hit)
            ranks.append(rank)
        below = (
            lax.broadcasted_iota(jnp.int32, (devices, devices), 1)
            < lax.broadcasted_iota(jnp.int32, (devices, devices), 0)
        ).astype(BF16)
        first = nn(below, jnp.broadcast_to(count, (devices, LANES)).astype(BF16))
        first_ref[...] = first.astype(jnp.int32)
        fixed = names.astype(F32) * capacity
        padded = []
        for c in range(rb_count):
            cut = slice(c * width, (c + 1) * width)
            rank = ranks[c] - 1.0
            place = jnp.sum(hits[c] * (rank + first[:, :1]), axis=0, keepdims=True)
            place_ref[:, cut] = place.astype(jnp.int32)
            slot = jnp.sum(hits[c] * (rank + fixed), axis=0, keepdims=True)
            padded.append(slot.astype(jnp.int32))
        padded = jnp.concatenate(padded, axis=1)
        surface = surface_ref[...]
        digit = lax.broadcasted_iota(jnp.int32, (8, rows), 0)
        digits = jnp.where(
            digit == 0, surface >> 8, jnp.where(digit == 1, surface & 255, 1)
        ).astype(F32).astype(BF16)

        def step(i, carry):
            wanted = lax.broadcasted_iota(jnp.int32, (width, rows), 0) + i * width
            chosen = jnp.where(padded == wanted, 1.0, 0.0).astype(BF16)
            found = nt(digits, chosen)
            label = jnp.where(found[2:3] > 0.5, found[0:1] * 256.0 + found[1:2], float(surfaces))
            cut = pl.ds(pl.multiple_of(i * width, width), width)
            label_ref[:, cut] = label.astype(jnp.int32)
            return carry

        lax.fori_loop(0, devices * capacity // width, step, 0)

    place, first, labels = local_kernel(
        route,
        (
            shape((1, rows), jnp.int32),
            shape((devices, LANES), jnp.int32),
            shape((1, devices * capacity), jnp.int32),
        ),
        [VMEM] * 2,
        flops=rows * devices * capacity * 4,
    )(patch_owner.reshape(1, rows), patch_surface.reshape(1, rows))
    first = first[:, 0]

    def pack_rows(
        first_ref,
        place_ref,
        got_ref,
        far_ref,
        adj_ref,
        zero_ref,
        one_ref,
        full_ref,
        send_ref,
        grad,
        ordered,
    ):
        for r in range(rb_count):
            b, w = of(full_ref, 1, r), of(full_ref, 2, r)
            a = adj_ref[r]
            value = (w + a + arrived(got_ref, far_ref, r)) * b - (w * one_ref[r] + a * zero_ref[r])
            high = value.astype(BF16).astype(F32)
            low = value - high
            both = jnp.concatenate([high] * pack + [low] * pack, axis=0)
            grad[:, r * width : (r + 1) * width] = both.astype(BF16)
        ordered[rows:] = jnp.zeros((capacity, LANES), F32)
        place_row = place_ref[...]

        def order(i, carry):
            wanted = lax.broadcasted_iota(jnp.int32, (width, rows), 0) + i * width
            chosen = jnp.where(place_row == wanted, 1.0, 0.0).astype(BF16)
            moved = nt(chosen, grad[...])
            cut = pl.ds(pl.multiple_of(i * width, width), width)
            ordered[cut] = moved[:, :LANES] + moved[:, LANES:]
            return carry

        lax.fori_loop(0, rb_count, order, 0)
        lane = lax.broadcasted_iota(jnp.int32, (share, LANES), 1) // bands

        def fill(o, carry):
            at = first_ref[o]
            value = ordered[pl.ds(at, share)]
            for q in range(1, pack):
                value = jnp.where(lane == q, ordered[pl.ds(at + q * share, share)], value)
            send_ref[o] = value
            return carry

        lax.fori_loop(0, devices, fill, 0)

    received = devices * share

    def choose(label_ref, chosen_ref, count_ref):
        ones = jnp.ones((8, received), BF16)

        def step(i, carry):
            wanted = lax.broadcasted_iota(jnp.int32, (LANES, received), 0) + i * LANES
            cut = pl.ds(pl.multiple_of(i * LANES, LANES), LANES)
            count = jnp.zeros((8, LANES), F32)
            for q in range(pack):
                chosen = jnp.where(label_ref[q : q + 1] == wanted, 1.0, 0.0).astype(BF16)
                chosen_ref[q, cut] = chosen
                count = count + nt(ones, chosen)
            count_ref[:, cut] = jnp.maximum(count, 1.0)
            return carry

        lax.fori_loop(0, surfaces // LANES, step, 0)

    def reduce_rows(chosen_ref, count_ref, got_ref, out_ref, parts):
        lane = lax.broadcasted_iota(jnp.int32, (received, LANES), 1) // bands
        value = got_ref[...]
        high = value.astype(BF16).astype(F32)
        low = value - high
        for q in range(pack):
            parts[q, :, :LANES] = jnp.where(lane == q, high, 0.0).astype(BF16)
            parts[q, :, LANES:] = jnp.where(lane == q, low, 0.0).astype(BF16)

        def step(i, carry):
            cut = pl.ds(pl.multiple_of(i * LANES, LANES), LANES)
            total = jnp.zeros((LANES, 2 * LANES), F32)
            for q in range(pack):
                total = total + nn(chosen_ref[q, cut], parts[q])
            turned = (total[:, :LANES] + total[:, LANES:]).T
            sums = turned[:bands]
            for q in range(1, pack):
                sums = sums + turned[q * bands : (q + 1) * bands]
            out_ref[:, cut] = sums / count_ref[:1, cut]
            return carry

        lax.fori_loop(0, surfaces // LANES, step, 0)

    own, near, far = local_kernel(
        adjoint_first, part_outs, [SMEM, VMEM, VMEM], part_scratch, flops=pass_flops
    )(slots, matrix, small)
    start = small[:, :per_group]
    start_in, start_out = inner(start), outer(start)
    got_one, far_one = collect(own, near, far)

    zero, rad = local_kernel(
        forward_first,
        (shape(block_shape, F32), shape(gathered_shape, BF16)),
        [SMEM] + [VMEM] * 5,
        window_scratch,
        flops=pass_flops,
    )(slots, matrix, start, start_in, start_out, full)
    rad = exchange(rad)
    rad_in, rad_out = inner(rad), outer(rad)

    adjoint_one, own, near, far = local_kernel(
        adjoint_second,
        (shape(block_shape, F32),) + part_outs,
        [SMEM] + [VMEM] * 4,
        part_scratch,
        flops=pass_flops,
    )(slots, matrix, got_one, far_one, full)
    got_zero, far_zero = collect(own, near, far)

    one, radiosity = local_kernel(
        forward_second,
        (shape(block_shape, F32), shape((bands, rows), F32)),
        [SMEM] + [VMEM] * 5,
        window_scratch,
        flops=pass_flops,
    )(slots, matrix, rad, rad_in, rad_out, full)

    labels = lax.all_to_all(labels.reshape(devices, capacity), ("band", "patch"), 0, 0, tiled=True)
    labels = jnp.swapaxes(labels.reshape(devices, pack, share), 0, 1).reshape(pack, received)
    chosen, counts = local_kernel(
        choose,
        (shape((pack, surfaces, received), BF16), shape((8, surfaces), F32)),
        [VMEM],
    )(labels)

    send = local_kernel(
        pack_rows,
        shape((devices, share, LANES), F32),
        [SMEM] + [VMEM] * 7,
        [pltpu.VMEM((2 * LANES, rows), BF16), pltpu.VMEM((rows + capacity, LANES), F32)],
    )(first, place, got_zero, far_zero, adjoint_one, zero, one, full)
    send = lax.all_to_all(send, ("band", "patch"), 0, 0, tiled=True)
    surface_grad = local_kernel(
        reduce_rows,
        shape((bands, surfaces), F32),
        [VMEM] * 3,
        [pltpu.VMEM((pack, received, 2 * LANES), BF16)],
    )(chosen, counts, send.reshape(received, LANES))
    return (radiosity.reshape(bands, 1, 1, rows), surface_grad)


def solution(mesh):
    in_specs = (
        P("band", "patch"),
        P("band", "patch"),
        P("band", "patch"),
        P("patch", "band", None, None, None, None),
        P("patch", "band", None, None),
        P("patch", "band", None, None),
        P("patch", "band", None),
    )
    out_specs = (P(None, "patch", "band", None), P(None, ("band", "patch")))
    return jax.shard_map(body, mesh=mesh, in_specs=in_specs, out_specs=out_specs, check_vma=False)
```

```python
import jax
import jax.numpy as jnp
from jax import lax
from jax.experimental import pallas as pl
from jax.experimental.pallas import tpu as pltpu
from jax.sharding import PartitionSpec as P

F32 = jnp.float32
BF16 = jnp.bfloat16
I32 = jnp.int32
LANES = 128
MIB = 1 << 20
VMEM = pl.BlockSpec(memory_space=pltpu.VMEM)
TOP = 32767.0


def shape(dims, dtype):
    return jax.ShapeDtypeStruct(dims, dtype)


def whole(dims):
    return pl.BlockSpec(dims, lambda i, *_: (0,) * len(dims))


def along(dims, axis):
    return pl.BlockSpec(dims, lambda i, *_: tuple(i if d == axis else 0 for d in range(len(dims))))


def nt(a, b):
    return lax.dot_general(a, b, (((1,), (1,)), ((), ())), preferred_element_type=F32)


def nn(a, b):
    return lax.dot_general(a, b, (((1,), (0,)), ((), ())), preferred_element_type=F32)


def iota(dims, axis):
    return lax.broadcasted_iota(I32, dims, axis)


def kernel_call(kernel, steps, scalars, ins, outs, args, scratch=(), limit=24 * MIB, flops=0):
    return pl.pallas_call(
        kernel,
        out_shape=[o for _, o in outs],
        grid_spec=pltpu.PrefetchScalarGridSpec(
            num_scalar_prefetch=scalars,
            grid=(steps,),
            in_specs=ins,
            out_specs=[s for s, _ in outs],
            scratch_shapes=scratch,
        ),
        compiler_params=pltpu.CompilerParams(vmem_limit_bytes=limit),
        cost_estimate=pl.CostEstimate(flops=flops, bytes_accessed=flops // 32, transcendentals=0),
    )(*args)


def body(
    emissivity, blackbody, loss_weights, view_blocks, column_blocks, patch_owner, patch_surface
):
    split = lax.axis_size("band")
    groups = lax.axis_size("patch")
    devices = split * groups
    part_bands = emissivity.shape[0]
    bands = part_bands * split
    rb_count, depth, width = view_blocks.shape[2:5]
    rows = rb_count * width
    per_group = split * rb_count
    capacity = max(2, 3 * rows // devices)
    surfaces = rows // 2
    me = lax.axis_index("patch")

    team_of = [(g, (g + 1) % groups) for g in range(1, groups, 2)]
    teams = [[b * groups + g for g in pair for b in range(split)] for pair in team_of]

    def place_in_team():
        return 1 - lax.axis_index("patch") % 2

    def inner(block):
        return lax.ppermute(block, "patch", [(i, i ^ 1) for i in range(groups)])

    def outer(block):
        return lax.ppermute(
            block, "patch", [(i, (i + (1 if i % 2 else -1)) % groups) for i in range(groups)]
        )

    def across(block, d):
        return lax.ppermute(block, "band", [(i, i ^ d) for i in range(split)])

    def team_exchange(block):
        return lax.all_to_all(
            block, ("band", "patch"), 0, 0, axis_index_groups=teams, tiled=True
        )

    columns = column_blocks.reshape(rb_count * depth)
    column_group = columns // per_group
    third = jnp.where(column_group == me, 0, jnp.where(column_group == (me ^ 1), 1, 2))
    slots = third * per_group + columns % per_group
    matrix = view_blocks.reshape(rb_count, depth, width, width)
    block_shape = (rb_count, bands, width)
    team_shape = (2 * split,) + block_shape
    part_shape = (split,) + block_shape
    pass_flops = 2 * bands * rb_count * depth * width * width
    once = rb_count // 4
    half = depth // 2

    def prepare(e_ref, b_ref, w_ref, start_ref, full_ref):
        for r in range(rb_count):
            cut = slice(r * width, (r + 1) * width)
            e, b, w = e_ref[:, cut], b_ref[:, cut], w_ref[:, cut]
            start = (e * b).astype(BF16)
            for d in range(2 * split):
                start_ref[d, r] = start
            full_ref[0, 0, r] = e
            full_ref[0, 1, r] = b
            full_ref[0, 2, r] = w

    piece = (3, rb_count, part_bands, width)
    start, full = kernel_call(
        prepare,
        split,
        0,
        [along((part_bands, rows), 1)] * 3,
        [
            (
                along((2 * split, rb_count, part_bands, width), 1),
                shape((2 * split, per_group, part_bands, width), BF16),
            ),
            (along((1,) + piece, 0), shape((split,) + piece, F32)),
        ],
        (emissivity, blackbody, loss_weights),
    )

    band = lax.axis_index("band")
    pieces = [
        across(lax.dynamic_index_in_dim(full, band ^ d, keepdims=False), d) if d else
        lax.dynamic_index_in_dim(full, band, keepdims=False)
        for d in range(split)
    ]
    start = team_exchange(start)

    def scatter_products(slots_ref, m_refs, value_of, outs, total):
        i = pl.program_id(0)

        @pl.when(i == 0)
        def _():
            total[...] = jnp.zeros_like(total)

        for q in range(once):
            u = value_of(q)
            for k in range(depth):
                s = slots_ref[(i * once + q) * depth + k]
                total[s] += nn(u, m_refs[k // half][q, k % half])

        @pl.when(i == pl.num_programs(0) - 1)
        def _():
            for third_index, out_ref in enumerate(outs):
                for s in range(split):
                    at = third_index * per_group + s * rb_count
                    out_ref[s] = total[at : at + rb_count].astype(out_ref.dtype)

    matrix_specs = [
        pl.BlockSpec((once, half, width, width), lambda i, *_, h=h: (i, h, 0, 0)) for h in (0, 1)
    ]
    part_outs = [(whole(part_shape), shape(part_shape, t)) for t in (F32, BF16, BF16)]
    total_scratch = [pltpu.VMEM((3 * per_group, bands, width), F32)]
    step_rows = along((once, bands, width), 0)
    full_rows = along((3, once, bands, width), 1)

    def adjoint_first(slots_ref, m0, m1, *refs):
        piece_refs, (full_ref, own_ref, near_ref, far_ref, total) = refs[:split], refs[split:]
        b = lax.axis_index("band")
        for d in range(split):
            at = pl.ds(pl.multiple_of((b ^ d) * part_bands, part_bands), part_bands)
            for a in range(3):
                for q in range(once):
                    full_ref[a, q, at, :] = piece_refs[d][a, q]

        def value_of(q):
            return ((1.0 - full_ref[0, q]) * full_ref[2, q]).astype(BF16)

        scatter_products(slots_ref, (m0, m1), value_of, (own_ref, near_ref, far_ref), total)

    def adjoint_second(slots_ref, m0, m1, got_ref, full_ref, one_ref, own_ref, near_ref, far_ref, total):
        def value_of(q):
            value = got_ref[0, q].astype(F32)
            for s in range(1, 2 * split):
                value = value + got_ref[s, q].astype(F32)
            one_ref[q] = value
            return ((1.0 - full_ref[0, q]) * value).astype(BF16)

        scatter_products(slots_ref, (m0, m1), value_of, (own_ref, near_ref, far_ref), total)

    def merge(own_ref, near_ref, far_ref, pay_ref):
        mine = place_in_team() * split
        for s in range(split):
            pay_ref[mine + s] = (own_ref[s] + near_ref[s].astype(F32)).astype(BF16)
            pay_ref[split - mine + s] = far_ref[s]

    def collect(own, near, far):
        (pay,) = kernel_call(
            merge,
            1,
            0,
            [whole(part_shape)] * 3,
            [(whole(team_shape), shape(team_shape, BF16))],
            (own, inner(near), far),
        )
        return team_exchange(pay)

    def products(slots_ref, m_refs, held, finish):
        i = pl.program_id(0)
        for q in range(once):
            value = jnp.zeros((bands, width), F32)
            for k in range(depth):
                s = slots_ref[(i * once + q) * depth + k]
                value = value + nt(held[s], m_refs[k // half][q, k % half])
            finish(q, value)

    def forward_first(slots_ref, m0, m1, team_ref, near_ref, full_ref, zero_ref, rad_ref, held):
        @pl.when(pl.program_id(0) == 0)
        def _():
            mine = place_in_team() * split

            def fill(c, carry):
                for third_index, (ref, first) in enumerate(
                    ((team_ref, mine), (near_ref, 0), (team_ref, split - mine))
                ):
                    parts = [ref[first + s, c].astype(F32) for s in range(split)]
                    held[third_index * per_group + c] = jnp.concatenate(parts, axis=0).astype(BF16)
                return carry

            lax.fori_loop(0, per_group, fill, 0)

        def finish(q, value):
            zero_ref[q] = value
            e, b = full_ref[0, q], full_ref[1, q]
            rad_ref[q] = (e * b + (1.0 - e) * value).astype(BF16)

        products(slots_ref, (m0, m1), held, finish)

    def forward_second(slots_ref, m0, m1, *refs):
        piece_refs, (full_ref, one_ref, rad_ref, held) = refs[:split], refs[split:]

        @pl.when(pl.program_id(0) == 0)
        def _():
            b = lax.axis_index("band")
            for d in range(split):
                for third_index in range(3):
                    at = third_index * per_group + (b ^ d) * rb_count
                    held[pl.ds(at, rb_count)] = piece_refs[d][third_index]

        def finish(q, value):
            one_ref[q] = value
            e, b = full_ref[0, q], full_ref[1, q]
            rad_ref[:, q * width : (q + 1) * width] = e * b + (1.0 - e) * value

        products(slots_ref, (m0, m1), held, finish)

    window_scratch = [pltpu.VMEM((3 * per_group, bands, width), BF16)]

    tail = max(0, capacity - LANES)
    seats = LANES + (LANES // 2 if tail else 0)
    value_rows = bands + (bands // 2 if tail else 0)
    send_rows = value_rows + 8

    def route(owner_ref, surface_ref, rank_ref, label_ref):
        names = iota((devices, width), 0)
        upper = (iota((width, width), 0) <= iota((width, width), 1)).astype(BF16)
        seat = iota((seats, width), 0)
        count = jnp.zeros((devices, 1), F32)
        found = jnp.zeros((3 * devices, seats), F32)
        for c in range(rb_count):
            cut = slice(c * width, (c + 1) * width)
            hit = (owner_ref[:, cut] == names).astype(F32)
            rank = nn(hit.astype(BF16), upper) + count
            count = rank[:, width - 1 : width]
            place = jnp.sum(hit * rank, axis=0, keepdims=True).astype(I32) - 1
            rank_ref[:, cut] = place
            seated = (seat == place).astype(F32).astype(BF16)
            surface = surface_ref[:, cut]
            high = (surface >> 7).astype(F32)
            low = (surface & 127).astype(F32)
            marks = jnp.concatenate([hit, hit * high, hit * low], axis=0).astype(BF16)
            found = found + nt(marks, seated)
        taken, high, low = (found[a * devices : (a + 1) * devices] for a in range(3))
        label_ref[...] = jnp.where(taken > 0.5, high * 128.0 + low, float(surfaces))

    rank, labels = kernel_call(
        route,
        1,
        0,
        [whole((1, rows))] * 2,
        [
            (whole((1, rows)), shape((1, rows), I32)),
            (whole((devices, seats)), shape((devices, seats), F32)),
        ],
        (patch_owner.reshape(1, rows), patch_surface.reshape(1, rows)),
    )

    owners_once = 4

    def pack_rows(
        got_ref, adj_ref, zero_ref, one_ref, full_ref, owner_ref, rank_ref, label_ref,
        send_ref, grad, digits, seated, most,
    ):
        i = pl.program_id(0)

        @pl.when(i == 0)
        def _():
            most[...] = jnp.full_like(most, 1e-30)

        for q in range(once):
            b, w = full_ref[1, q], full_ref[2, q]
            a = adj_ref[q]
            last = got_ref[0, q].astype(F32)
            for s in range(1, 2 * split):
                last = last + got_ref[s, q].astype(F32)
            value = (w + a + last) * b - (w * one_ref[q] + a * zero_ref[q])
            cut = pl.ds(pl.multiple_of((i * once + q) * width, width), width)
            grad[:, cut] = value
            most[...] = jnp.maximum(most[...], jnp.max(jnp.abs(value), axis=1, keepdims=True))

        @pl.when(i == pl.num_programs(0) - 1)
        def _():
            power = jnp.floor(jnp.log2(most[...])) - 14.0
            power = jnp.where(most[...] * jnp.exp2(-power) > TOP, power + 1.0, power)
            scale = jnp.exp2(-power)[:, :1]
            ordinal = jnp.round(jnp.clip(grad[...] * scale, -TOP, TOP))
            high = ordinal.astype(BF16)
            digits[:bands] = high
            digits[bands:] = (ordinal - high.astype(F32)).astype(BF16)
            seated[...] = (iota((seats, rows), 0) == rank_ref[...]).astype(F32).astype(BF16)
            powers = power.T[:1]
            powers = jnp.concatenate([powers, jnp.zeros((1, LANES - bands), F32)], axis=1)

            def step(c, carry):
                hits = []
                for j in range(owners_once):
                    hit = (owner_ref[...] == c * owners_once + j).astype(F32).astype(BF16)
                    hits.append(digits[...] * hit)
                moved = nt(jnp.concatenate(hits, axis=0), seated[...])
                for j in range(owners_once):
                    at = 2 * bands * j
                    block = moved[at : at + bands] + moved[at + bands : at + 2 * bands]
                    label = label_ref[pl.ds(c * owners_once + j, 1)]
                    parts = [block[:, :LANES]]
                    extra = [label[:, :LANES]]
                    if tail:
                        over = block[:, LANES:]
                        parts.append(
                            jnp.concatenate([over[: bands // 2], over[bands // 2 :]], axis=1)
                        )
                        over = label[:, LANES:]
                        extra.append(jnp.concatenate([over, over], axis=1))
                    else:
                        extra.append(jnp.zeros((1, LANES), F32))
                    extra.append(powers)
                    extra.append(jnp.zeros((5, LANES), F32))
                    out = jnp.concatenate(parts + [jnp.concatenate(extra, axis=0)], axis=0)
                    send_ref[c * owners_once + j] = out.astype(I32).astype(jnp.int16)
                return carry

            lax.fori_loop(0, devices // owners_once, step, 0)

    sources_once = 4
    tops = surfaces // LANES
    lot = sources_once * LANES * (2 if tail else 1)
    top_rows = 2 * bands + 16

    def reduce_rows(got_ref, out_ref, scales, total):
        power = got_ref[:, value_rows + 2].astype(F32)
        scale = jnp.exp2(power).T[:bands]
        for s in range(devices):
            scales[s] = jnp.broadcast_to(scale[:, s : s + 1], (bands, LANES))
        total[...] = jnp.zeros_like(total)
        left = iota((bands // 2, LANES), 1) < LANES // 2
        first_half = iota((1, LANES), 1) < LANES // 2

        def step(c, carry):
            values, labels, once_each = [], [], []
            for j in range(sources_once):
                source = c * sources_once + j
                got = got_ref[source].astype(F32)
                grown = scales[source]
                values.append(got[:bands] * grown)
                labels.append(got[value_rows : value_rows + 1])
                once_each.append(jnp.ones((1, LANES), F32))
                if tail:
                    over = got[bands:value_rows]
                    low = jnp.where(left, over * grown[: bands // 2], 0.0)
                    high = jnp.where(left, 0.0, over * grown[bands // 2 :])
                    values.append(jnp.concatenate([low, high], axis=0))
                    labels.append(got[value_rows + 1 : value_rows + 2])
                    once_each.append(jnp.where(first_half, 1.0, 0.0))
            value = jnp.concatenate(values, axis=1)
            label = jnp.concatenate(labels, axis=1).astype(I32)
            counted = jnp.concatenate(once_each, axis=1)
            high = value.astype(BF16)
            low = (value - high.astype(F32)).astype(BF16)
            counted = jnp.broadcast_to(counted, (16, lot)).astype(BF16)
            both = jnp.concatenate([high, low, counted], axis=0)
            seated = (iota((LANES, lot), 0) == (label & 127)).astype(F32).astype(BF16)
            chosen = [both * (label >> 7 == t).astype(F32).astype(BF16) for t in range(tops)]
            total[...] += nt(jnp.concatenate(chosen, axis=0), seated)
            return carry

        lax.fori_loop(0, devices // sources_once, step, 0)
        for t in range(tops):
            at = t * top_rows
            sums = total[at : at + bands] + total[at + bands : at + 2 * bands]
            count = jnp.maximum(total[at + 2 * bands : at + 2 * bands + 1], 1.0)
            out_ref[:, t * LANES : (t + 1) * LANES] = sums / count

    full, own, near, far = kernel_call(
        adjoint_first,
        4,
        1,
        matrix_specs + [along((3, once, part_bands, width), 1)] * split,
        [(full_rows, shape((3,) + block_shape, F32))] + part_outs,
        (slots, matrix, matrix) + tuple(pieces),
        total_scratch,
        flops=pass_flops,
    )
    got_one = collect(own, near, far)

    mine = (1 - me % 2) * split
    start_near = inner(lax.dynamic_slice_in_dim(start, mine, split, axis=0))
    zero, rad = kernel_call(
        forward_first,
        4,
        1,
        matrix_specs + [whole(start.shape), whole(start_near.shape), full_rows],
        [(step_rows, shape(block_shape, F32)), (step_rows, shape(block_shape, BF16))],
        (slots, matrix, matrix, start, start_near, full),
        window_scratch,
        flops=pass_flops,
    )
    rad = jnp.stack([rad, inner(rad), outer(rad)])
    rads = [rad] + [across(rad, d) for d in range(1, split)]

    adjoint_one, own, near, far = kernel_call(
        adjoint_second,
        4,
        1,
        matrix_specs + [along((2 * split, once, bands, width), 1), full_rows],
        [(step_rows, shape(block_shape, F32))] + part_outs,
        (slots, matrix, matrix, got_one, full),
        total_scratch,
        flops=pass_flops,
    )
    got_zero = collect(own, near, far)

    one, radiosity = kernel_call(
        forward_second,
        4,
        1,
        matrix_specs + [whole((3,) + block_shape)] * split + [full_rows],
        [
            (step_rows, shape(block_shape, F32)),
            (along((bands, once * width), 1), shape((bands, rows), F32)),
        ],
        (slots, matrix, matrix) + tuple(rads) + (full,),
        window_scratch,
        flops=pass_flops,
    )

    (send,) = kernel_call(
        pack_rows,
        4,
        0,
        [along((2 * split, once, bands, width), 1)]
        + [step_rows] * 3
        + [full_rows, whole((1, rows)), whole((1, rows)), whole((devices, seats))],
        [
            (
                whole((devices, send_rows, LANES)),
                shape((devices, send_rows, LANES), jnp.int16),
            )
        ],
        (
            got_zero,
            adjoint_one,
            zero,
            one,
            full,
            patch_owner.reshape(1, rows),
            rank,
            labels,
        ),
        [
            pltpu.VMEM((bands, rows), F32),
            pltpu.VMEM((2 * bands, rows), BF16),
            pltpu.VMEM((seats, rows), BF16),
            pltpu.VMEM((bands, LANES), F32),
        ],
    )
    send = lax.all_to_all(send, ("band", "patch"), 0, 0, tiled=True)
    (surface_grad,) = kernel_call(
        reduce_rows,
        1,
        0,
        [whole((devices, send_rows, LANES))],
        [(whole((bands, surfaces)), shape((bands, surfaces), F32))],
        (send,),
        [
            pltpu.VMEM((devices, bands, LANES), F32),
            pltpu.VMEM((tops * top_rows, LANES), F32),
        ],
    )
    return (radiosity.reshape(bands, 1, 1, rows), surface_grad)


def solution(mesh):
    in_specs = (
        P("band", "patch"),
        P("band", "patch"),
        P("band", "patch"),
        P("patch", "band", None, None, None, None),
        P("patch", "band", None, None),
        P("patch", "band", None, None),
        P("patch", "band", None),
    )
    out_specs = (P(None, "patch", "band", None), P(None, ("band", "patch")))
    return jax.shard_map(body, mesh=mesh, in_specs=in_specs, out_specs=out_specs, check_vma=False)
```

```python
import jax
import jax.numpy as jnp
from jax import lax
from jax.experimental import pallas as pl
from jax.experimental.pallas import tpu as pltpu
from jax.sharding import PartitionSpec as P

F32 = jnp.float32
BF16 = jnp.bfloat16
I32 = jnp.int32
LANES = 128
MIB = 1 << 20
VMEM = pl.BlockSpec(memory_space=pltpu.VMEM)
TOP = 32767.0


def shape(dims, dtype):
    return jax.ShapeDtypeStruct(dims, dtype)


def whole(dims):
    return pl.BlockSpec(dims, lambda i, *_: (0,) * len(dims))


def along(dims, axis):
    return pl.BlockSpec(dims, lambda i, *_: tuple(i if d == axis else 0 for d in range(len(dims))))


def nt(a, b):
    return lax.dot_general(a, b, (((1,), (1,)), ((), ())), preferred_element_type=F32)


def nn(a, b):
    return lax.dot_general(a, b, (((1,), (0,)), ((), ())), preferred_element_type=F32)


def iota(dims, axis):
    return lax.broadcasted_iota(I32, dims, axis)


def kernel_call(kernel, steps, scalars, ins, outs, args, scratch=(), limit=50 * MIB, flops=0):
    return pl.pallas_call(
        kernel,
        out_shape=[o for _, o in outs],
        grid_spec=pltpu.PrefetchScalarGridSpec(
            num_scalar_prefetch=scalars,
            grid=(steps,),
            in_specs=ins,
            out_specs=[s for s, _ in outs],
            scratch_shapes=scratch,
        ),
        compiler_params=pltpu.CompilerParams(vmem_limit_bytes=limit),
        cost_estimate=pl.CostEstimate(flops=flops, bytes_accessed=flops // 32, transcendentals=0),
    )(*args)


def body(
    emissivity, blackbody, loss_weights, view_blocks, column_blocks, patch_owner, patch_surface
):
    split = lax.axis_size("band")
    groups = lax.axis_size("patch")
    devices = split * groups
    part_bands = emissivity.shape[0]
    bands = part_bands * split
    rb_count, depth, width = view_blocks.shape[2:5]
    rows = rb_count * width
    per_group = split * rb_count
    capacity = max(2, 3 * rows // devices)
    surfaces = rows // 2
    me = lax.axis_index("patch")

    team_of = [(g, (g + 1) % groups) for g in range(1, groups, 2)]
    teams = [[b * groups + g for g in pair for b in range(split)] for pair in team_of]

    def place_in_team():
        return 1 - lax.axis_index("patch") % 2

    def inner(block):
        return lax.ppermute(block, "patch", [(i, i ^ 1) for i in range(groups)])

    def outer(block):
        return lax.ppermute(
            block, "patch", [(i, (i + (1 if i % 2 else -1)) % groups) for i in range(groups)]
        )

    def across(block, d):
        return lax.ppermute(block, "band", [(i, i ^ d) for i in range(split)])

    def team_exchange(block):
        return lax.all_to_all(
            block, ("band", "patch"), 0, 0, axis_index_groups=teams, tiled=True
        )

    columns = column_blocks.reshape(rb_count * depth)
    column_group = columns // per_group
    third = jnp.where(column_group == me, 0, jnp.where(column_group == (me ^ 1), 1, 2))
    slots = third * per_group + columns % per_group
    matrix = view_blocks.reshape(rb_count, depth, width, width)
    block_shape = (rb_count, bands, width)
    team_shape = (2 * split,) + block_shape
    part_shape = (split,) + block_shape
    pass_flops = 2 * bands * rb_count * depth * width * width
    once = rb_count // 4
    half = depth // 2

    def prepare(e_ref, b_ref, w_ref, start_ref, full_ref):
        for r in range(rb_count):
            cut = slice(r * width, (r + 1) * width)
            e, b, w = e_ref[:, cut], b_ref[:, cut], w_ref[:, cut]
            start = (e * b).astype(BF16)
            for d in range(2 * split):
                start_ref[d, r] = start
            full_ref[0, 0, r] = e
            full_ref[0, 1, r] = b
            full_ref[0, 2, r] = w

    piece = (3, rb_count, part_bands, width)
    start, full = kernel_call(
        prepare,
        split,
        0,
        [along((part_bands, rows), 1)] * 3,
        [
            (
                along((2 * split, rb_count, part_bands, width), 1),
                shape((2 * split, per_group, part_bands, width), BF16),
            ),
            (along((1,) + piece, 0), shape((split,) + piece, F32)),
        ],
        (emissivity, blackbody, loss_weights),
        limit=60 * MIB,
    )

    band = lax.axis_index("band")
    pieces = [
        across(lax.dynamic_index_in_dim(full, band ^ d, keepdims=False), d) if d else
        lax.dynamic_index_in_dim(full, band, keepdims=False)
        for d in range(split)
    ]
    start = team_exchange(start)

    def scatter_products(slots_ref, m_refs, value_of, outs, total):
        i = pl.program_id(0)

        @pl.when(i == 0)
        def _():
            total[...] = jnp.zeros_like(total)

        for q in range(once):
            u = value_of(q)
            for k in range(depth):
                s = slots_ref[(i * once + q) * depth + k]
                total[s] += nn(u, m_refs[k // half][q, k % half])

        @pl.when(i == pl.num_programs(0) - 1)
        def _():
            for third_index, out_ref in enumerate(outs):
                for s in range(split):
                    at = third_index * per_group + s * rb_count
                    out_ref[s] = total[at : at + rb_count].astype(out_ref.dtype)

    matrix_specs = [
        pl.BlockSpec((once, half, width, width), lambda i, *_, h=h: (i, h, 0, 0)) for h in (0, 1)
    ]
    part_outs = [(whole(part_shape), shape(part_shape, t)) for t in (F32, BF16, BF16)]
    total_scratch = [pltpu.VMEM((3 * per_group, bands, width), F32)]
    step_rows = along((once, bands, width), 0)
    full_rows = along((3, once, bands, width), 1)

    def adjoint_first(slots_ref, m0, m1, *refs):
        piece_refs, (full_ref, own_ref, near_ref, far_ref, total) = refs[:split], refs[split:]
        b = lax.axis_index("band")
        for d in range(split):
            at = pl.ds(pl.multiple_of((b ^ d) * part_bands, part_bands), part_bands)
            for a in range(3):
                for q in range(once):
                    full_ref[a, q, at, :] = piece_refs[d][a, q]

        def value_of(q):
            return ((1.0 - full_ref[0, q]) * full_ref[2, q]).astype(BF16)

        scatter_products(slots_ref, (m0, m1), value_of, (own_ref, near_ref, far_ref), total)

    def adjoint_second(slots_ref, m0, m1, got_ref, full_ref, one_ref, own_ref, near_ref, far_ref, total):
        def value_of(q):
            value = got_ref[0, q].astype(F32)
            for s in range(1, 2 * split):
                value = value + got_ref[s, q].astype(F32)
            one_ref[q] = value
            return ((1.0 - full_ref[0, q]) * value).astype(BF16)

        scatter_products(slots_ref, (m0, m1), value_of, (own_ref, near_ref, far_ref), total)

    def merge(own_ref, near_ref, far_ref, pay_ref):
        mine = place_in_team() * split
        for s in range(split):
            pay_ref[mine + s] = (own_ref[s] + near_ref[s].astype(F32)).astype(BF16)
            pay_ref[split - mine + s] = far_ref[s]

    def collect(own, near, far, before=None):
        (pay,) = kernel_call(
            merge,
            1,
            0,
            [whole(part_shape)] * 3,
            [(whole(team_shape), shape(team_shape, BF16))],
            (own, inner(near), far),
        )
        if before is not None:
            pay, _ = lax.optimization_barrier((pay, before))
        return team_exchange(pay)

    def products(slots_ref, m_refs, held, finish):
        i = pl.program_id(0)
        for q in range(once):
            value = jnp.zeros((bands, width), F32)
            for k in range(depth):
                s = slots_ref[(i * once + q) * depth + k]
                value = value + nt(held[s], m_refs[k // half][q, k % half])
            finish(q, value)

    def forward_first(slots_ref, m0, m1, team_ref, near_ref, full_ref, zero_ref, rad_ref, held):
        @pl.when(pl.program_id(0) == 0)
        def _():
            mine = place_in_team() * split

            def fill(c, carry):
                for third_index, (ref, first) in enumerate(
                    ((team_ref, mine), (near_ref, 0), (team_ref, split - mine))
                ):
                    parts = [ref[first + s, c].astype(F32) for s in range(split)]
                    held[third_index * per_group + c] = jnp.concatenate(parts, axis=0).astype(BF16)
                return carry

            lax.fori_loop(0, per_group, fill, 0)

        def finish(q, value):
            zero_ref[q] = value
            e, b = full_ref[0, q], full_ref[1, q]
            rad_ref[q] = (e * b + (1.0 - e) * value).astype(BF16)

        products(slots_ref, (m0, m1), held, finish)

    def forward_second(slots_ref, m0, m1, *refs):
        piece_refs, (full_ref, one_ref, rad_ref, held) = refs[:split], refs[split:]

        @pl.when(pl.program_id(0) == 0)
        def _():
            b = lax.axis_index("band")
            for d in range(split):
                for third_index in range(3):
                    at = third_index * per_group + (b ^ d) * rb_count
                    held[pl.ds(at, rb_count)] = piece_refs[d][third_index]

        def finish(q, value):
            one_ref[q] = value
            e, b = full_ref[0, q], full_ref[1, q]
            rad_ref[:, q * width : (q + 1) * width] = e * b + (1.0 - e) * value

        products(slots_ref, (m0, m1), held, finish)

    window_scratch = [pltpu.VMEM((3 * per_group, bands, width), BF16)]

    tail = max(0, capacity - LANES)
    seats = LANES + (LANES // 2 if tail else 0)
    value_rows = bands + (bands // 2 if tail else 0)
    send_rows = value_rows + 8

    def route(owner_ref, surface_ref, rank_ref, label_ref):
        names = iota((devices, width), 0)
        upper = (iota((width, width), 0) <= iota((width, width), 1)).astype(BF16)
        seat = iota((seats, width), 0)
        count = jnp.zeros((devices, 1), F32)
        found = jnp.zeros((3 * devices, seats), F32)
        for c in range(rb_count):
            cut = slice(c * width, (c + 1) * width)
            hit = (owner_ref[:, cut] == names).astype(F32)
            rank = nn(hit.astype(BF16), upper) + count
            count = rank[:, width - 1 : width]
            place = jnp.sum(hit * rank, axis=0, keepdims=True).astype(I32) - 1
            rank_ref[:, cut] = place
            seated = (seat == place).astype(F32).astype(BF16)
            surface = surface_ref[:, cut]
            high = (surface >> 7).astype(F32)
            low = (surface & 127).astype(F32)
            marks = jnp.concatenate([hit, hit * high, hit * low], axis=0).astype(BF16)
            found = found + nt(marks, seated)
        taken, high, low = (found[a * devices : (a + 1) * devices] for a in range(3))
        label_ref[...] = jnp.where(taken > 0.5, high * 128.0 + low, float(surfaces))

    rank, labels = kernel_call(
        route,
        1,
        0,
        [whole((1, rows))] * 2,
        [
            (whole((1, rows)), shape((1, rows), I32)),
            (whole((devices, seats)), shape((devices, seats), F32)),
        ],
        (patch_owner.reshape(1, rows), patch_surface.reshape(1, rows)),
    )

    owners_once = 4

    def pack_rows(
        got_ref, adj_ref, zero_ref, one_ref, full_ref, owner_ref, rank_ref, label_ref,
        send_ref, grad, digits, seated, most,
    ):
        i = pl.program_id(0)

        @pl.when(i == 0)
        def _():
            most[...] = jnp.full_like(most, 1e-30)

        for q in range(once):
            b, w = full_ref[1, q], full_ref[2, q]
            a = adj_ref[q]
            last = got_ref[0, q].astype(F32)
            for s in range(1, 2 * split):
                last = last + got_ref[s, q].astype(F32)
            value = (w + a + last) * b - (w * one_ref[q] + a * zero_ref[q])
            cut = pl.ds(pl.multiple_of((i * once + q) * width, width), width)
            grad[:, cut] = value
            most[...] = jnp.maximum(most[...], jnp.max(jnp.abs(value), axis=1, keepdims=True))

        @pl.when(i == pl.num_programs(0) - 1)
        def _():
            power = jnp.floor(jnp.log2(most[...])) - 14.0
            power = jnp.where(most[...] * jnp.exp2(-power) > TOP, power + 1.0, power)
            scale = jnp.exp2(-power)[:, :1]
            ordinal = jnp.round(jnp.clip(grad[...] * scale, -TOP, TOP))
            high = ordinal.astype(BF16)
            digits[:bands] = high
            digits[bands:] = (ordinal - high.astype(F32)).astype(BF16)
            seated[...] = (iota((seats, rows), 0) == rank_ref[...]).astype(F32).astype(BF16)
            powers = power.T[:1]
            powers = jnp.concatenate([powers, jnp.zeros((1, LANES - bands), F32)], axis=1)

            def step(c, carry):
                hits = []
                for j in range(owners_once):
                    hit = (owner_ref[...] == c * owners_once + j).astype(F32).astype(BF16)
                    hits.append(digits[...] * hit)
                moved = nt(jnp.concatenate(hits, axis=0), seated[...])
                for j in range(owners_once):
                    at = 2 * bands * j
                    block = moved[at : at + bands] + moved[at + bands : at + 2 * bands]
                    label = label_ref[pl.ds(c * owners_once + j, 1)]
                    parts = [block[:, :LANES]]
                    extra = [label[:, :LANES]]
                    if tail:
                        over = block[:, LANES:]
                        parts.append(
                            jnp.concatenate([over[: bands // 2], over[bands // 2 :]], axis=1)
                        )
                        over = label[:, LANES:]
                        extra.append(jnp.concatenate([over, over], axis=1))
                    else:
                        extra.append(jnp.zeros((1, LANES), F32))
                    extra.append(powers)
                    extra.append(jnp.zeros((5, LANES), F32))
                    out = jnp.concatenate(parts + [jnp.concatenate(extra, axis=0)], axis=0)
                    send_ref[c * owners_once + j] = out.astype(I32).astype(jnp.int16)
                return carry

            lax.fori_loop(0, devices // owners_once, step, 0)

    sources_once = 4
    tops = surfaces // LANES
    lot = sources_once * LANES * (2 if tail else 1)
    top_rows = 2 * bands + 16

    def reduce_rows(got_ref, out_ref, scales, total):
        power = got_ref[:, value_rows + 2].astype(F32)
        scale = jnp.exp2(power).T[:bands]
        for s in range(devices):
            scales[s] = jnp.broadcast_to(scale[:, s : s + 1], (bands, LANES))
        total[...] = jnp.zeros_like(total)
        left = iota((bands // 2, LANES), 1) < LANES // 2
        first_half = iota((1, LANES), 1) < LANES // 2

        def step(c, carry):
            values, labels, once_each = [], [], []
            for j in range(sources_once):
                source = c * sources_once + j
                got = got_ref[source].astype(F32)
                grown = scales[source]
                values.append(got[:bands] * grown)
                labels.append(got[value_rows : value_rows + 1])
                once_each.append(jnp.ones((1, LANES), F32))
                if tail:
                    over = got[bands:value_rows]
                    low = jnp.where(left, over * grown[: bands // 2], 0.0)
                    high = jnp.where(left, 0.0, over * grown[bands // 2 :])
                    values.append(jnp.concatenate([low, high], axis=0))
                    labels.append(got[value_rows + 1 : value_rows + 2])
                    once_each.append(jnp.where(first_half, 1.0, 0.0))
            value = jnp.concatenate(values, axis=1)
            label = jnp.concatenate(labels, axis=1).astype(I32)
            counted = jnp.concatenate(once_each, axis=1)
            high = value.astype(BF16)
            low = (value - high.astype(F32)).astype(BF16)
            counted = jnp.broadcast_to(counted, (16, lot)).astype(BF16)
            both = jnp.concatenate([high, low, counted], axis=0)
            seated = (iota((LANES, lot), 0) == (label & 127)).astype(F32).astype(BF16)
            chosen = [both * (label >> 7 == t).astype(F32).astype(BF16) for t in range(tops)]
            total[...] += nt(jnp.concatenate(chosen, axis=0), seated)
            return carry

        lax.fori_loop(0, devices // sources_once, step, 0)
        for t in range(tops):
            at = t * top_rows
            sums = total[at : at + bands] + total[at + bands : at + 2 * bands]
            count = jnp.maximum(total[at + 2 * bands : at + 2 * bands + 1], 1.0)
            out_ref[:, t * LANES : (t + 1) * LANES] = sums / count

    slots, rank, labels = lax.optimization_barrier((slots, rank, labels))
    full, own, near, far = kernel_call(
        adjoint_first,
        4,
        1,
        matrix_specs + [along((3, once, part_bands, width), 1)] * split,
        [(full_rows, shape((3,) + block_shape, F32))] + part_outs,
        (slots, matrix, matrix) + tuple(pieces),
        total_scratch,
        flops=pass_flops,
    )
    got_one = collect(own, near, far, start)

    mine = (1 - me % 2) * split
    start_near = inner(lax.dynamic_slice_in_dim(start, mine, split, axis=0))
    zero, rad = kernel_call(
        forward_first,
        4,
        1,
        matrix_specs + [whole(start.shape), whole(start_near.shape), full_rows],
        [(step_rows, shape(block_shape, F32)), (step_rows, shape(block_shape, BF16))],
        (slots, matrix, matrix, start, start_near, full),
        window_scratch,
        flops=pass_flops,
    )
    rad = jnp.stack([rad, inner(rad), outer(rad)])
    got_one, _ = lax.optimization_barrier((got_one, rad))

    adjoint_one, own, near, far = kernel_call(
        adjoint_second,
        4,
        1,
        matrix_specs + [along((2 * split, once, bands, width), 1), full_rows],
        [(step_rows, shape(block_shape, F32))] + part_outs,
        (slots, matrix, matrix, got_one, full),
        total_scratch,
        flops=pass_flops,
    )
    got_zero = collect(own, near, far)

    rads = [rad] + [across(rad, d) for d in range(1, split)]
    one, radiosity = kernel_call(
        forward_second,
        4,
        1,
        matrix_specs + [whole((3,) + block_shape)] * split + [full_rows],
        [
            (step_rows, shape(block_shape, F32)),
            (along((bands, once * width), 1), shape((bands, rows), F32)),
        ],
        (slots, matrix, matrix) + tuple(rads) + (full,),
        window_scratch,
        flops=pass_flops,
    )

    (send,) = kernel_call(
        pack_rows,
        4,
        0,
        [along((2 * split, once, bands, width), 1)]
        + [step_rows] * 3
        + [full_rows, whole((1, rows)), whole((1, rows)), whole((devices, seats))],
        [
            (
                whole((devices, send_rows, LANES)),
                shape((devices, send_rows, LANES), jnp.int16),
            )
        ],
        (
            got_zero,
            adjoint_one,
            zero,
            one,
            full,
            patch_owner.reshape(1, rows),
            rank,
            labels,
        ),
        [
            pltpu.VMEM((bands, rows), F32),
            pltpu.VMEM((2 * bands, rows), BF16),
            pltpu.VMEM((seats, rows), BF16),
            pltpu.VMEM((bands, LANES), F32),
        ],
    )
    send = lax.all_to_all(send, ("band", "patch"), 0, 0, tiled=True)
    (surface_grad,) = kernel_call(
        reduce_rows,
        1,
        0,
        [whole((devices, send_rows, LANES))],
        [(whole((bands, surfaces)), shape((bands, surfaces), F32))],
        (send,),
        [
            pltpu.VMEM((devices, bands, LANES), F32),
            pltpu.VMEM((tops * top_rows, LANES), F32),
        ],
    )
    return (radiosity.reshape(bands, 1, 1, rows), surface_grad)


def solution(mesh):
    in_specs = (
        P("band", "patch"),
        P("band", "patch"),
        P("band", "patch"),
        P("patch", "band", None, None, None, None),
        P("patch", "band", None, None),
        P("patch", "band", None, None),
        P("patch", "band", None),
    )
    out_specs = (P(None, "patch", "band", None), P(None, ("band", "patch")))
    return jax.shard_map(body, mesh=mesh, in_specs=in_specs, out_specs=out_specs, check_vma=False)
```

```python
import jax
import jax.numpy as jnp
from jax import lax
from jax.experimental import pallas as pl
from jax.experimental.pallas import tpu as pltpu
from jax.sharding import PartitionSpec as P

F32 = jnp.float32
BF16 = jnp.bfloat16
I32 = jnp.int32
LANES = 128
MIB = 1 << 20
VMEM = pl.BlockSpec(memory_space=pltpu.VMEM)
TOP = 32767.0


def shape(dims, dtype):
    return jax.ShapeDtypeStruct(dims, dtype)


def whole(dims):
    return pl.BlockSpec(dims, lambda i, *_: (0,) * len(dims))


def along(dims, axis):
    return pl.BlockSpec(dims, lambda i, *_: tuple(i if d == axis else 0 for d in range(len(dims))))


def nt(a, b):
    return lax.dot_general(a, b, (((1,), (1,)), ((), ())), preferred_element_type=F32)


def nn(a, b):
    return lax.dot_general(a, b, (((1,), (0,)), ((), ())), preferred_element_type=F32)


def iota(dims, axis):
    return lax.broadcasted_iota(I32, dims, axis)


def kernel_call(kernel, steps, scalars, ins, outs, args, scratch=(), limit=50 * MIB, flops=0):
    return pl.pallas_call(
        kernel,
        out_shape=[o for _, o in outs],
        grid_spec=pltpu.PrefetchScalarGridSpec(
            num_scalar_prefetch=scalars,
            grid=(steps,),
            in_specs=ins,
            out_specs=[s for s, _ in outs],
            scratch_shapes=scratch,
        ),
        compiler_params=pltpu.CompilerParams(vmem_limit_bytes=limit),
        cost_estimate=pl.CostEstimate(flops=flops, bytes_accessed=flops // 32, transcendentals=0),
    )(*args)


def body(
    emissivity, blackbody, loss_weights, view_blocks, column_blocks, patch_owner, patch_surface
):
    split = lax.axis_size("band")
    groups = lax.axis_size("patch")
    devices = split * groups
    part_bands = emissivity.shape[0]
    bands = part_bands * split
    rb_count, depth, width = view_blocks.shape[2:5]
    rows = rb_count * width
    per_group = split * rb_count
    capacity = max(2, 3 * rows // devices)
    surfaces = rows // 2
    me = lax.axis_index("patch")

    def inner(block):
        return lax.ppermute(block, "patch", [(i, i ^ 1) for i in range(groups)])

    def outer(block):
        return lax.ppermute(
            block, "patch", [(i, (i + (1 if i % 2 else -1)) % groups) for i in range(groups)]
        )

    def across(block, d):
        return lax.ppermute(block, "band", [(i, i ^ d) for i in range(split)])

    def outer_across(block, d):
        route = []
        for i in range(split):
            for g in range(groups):
                beyond = (g + (1 if g % 2 else -1)) % groups
                route.append((i * groups + g, (i ^ d) * groups + beyond))
        return lax.ppermute(block, ("band", "patch"), route)

    columns = column_blocks.reshape(rb_count * depth)
    column_group = columns // per_group
    third = jnp.where(column_group == me, 0, jnp.where(column_group == (me ^ 1), 1, 2))
    slots = third * per_group + columns % per_group
    matrix = view_blocks.reshape(rb_count, depth, width, width)
    block_shape = (rb_count, bands, width)
    part_shape = (split,) + block_shape
    pass_flops = 2 * bands * rb_count * depth * width * width
    once = rb_count // 4
    half = depth // 2

    def prepare(e_ref, b_ref, w_ref, start_ref, *piece_refs):
        band = lax.axis_index("band")
        for c in range(per_group):
            cut = slice(c * width, (c + 1) * width)
            start_ref[c] = (e_ref[:, cut] * b_ref[:, cut]).astype(BF16)
        for d in range(split):
            cut = pl.ds(pl.multiple_of((band ^ d) * rows, rows), rows)
            for a, ref in enumerate((e_ref, b_ref, w_ref)):
                piece_refs[d][a] = ref[:, cut]

    piece = (3, part_bands, rows)
    start_shape = (per_group, part_bands, width)
    start, *pieces = kernel_call(
        prepare,
        1,
        0,
        [whole((part_bands, per_group * width))] * 3,
        [(whole(start_shape), shape(start_shape, BF16))]
        + [(whole(piece), shape(piece, F32))] * split,
        (emissivity, blackbody, loss_weights),
        limit=60 * MIB,
    )
    pieces = [across(pieces[d], d) if d else pieces[d] for d in range(split)]

    def pair_of(block):
        return jnp.stack([block, outer(block)])

    def gather(pair, after):
        pairs = [pair] + [across(pair, d) for d in range(1, split)]
        pairs, _ = lax.optimization_barrier((pairs, after))
        return pairs + [inner(jnp.stack([p[0] for p in pairs]))]

    def scatter_products(slots_ref, m_refs, value_of, outs, total):
        i = pl.program_id(0)

        @pl.when(i == 0)
        def _():
            total[...] = jnp.zeros_like(total)

        for q in range(once):
            u = value_of(q)
            for k in range(depth):
                s = slots_ref[(i * once + q) * depth + k]
                total[s] += nn(u, m_refs[k // half][q, k % half])

        @pl.when(i == pl.num_programs(0) - 1)
        def _():
            own_ref, near_ref, *far_refs = outs
            band = lax.axis_index("band")
            for d in range(split):
                at = (band ^ d) * rb_count
                own_ref[d] = total[pl.ds(at, rb_count)]
                near_ref[d] = total[pl.ds(per_group + at, rb_count)].astype(BF16)
                far_refs[d][...] = total[pl.ds(2 * per_group + at, rb_count)].astype(BF16)

    matrix_specs = [
        pl.BlockSpec((once, half, width, width), lambda i, *_, h=h: (i, h, 0, 0)) for h in (0, 1)
    ]
    part_outs = [(whole(part_shape), shape(part_shape, t)) for t in (F32, BF16)]
    part_outs += [(whole(block_shape), shape(block_shape, BF16))] * split
    total_scratch = [pltpu.VMEM((3 * per_group, bands, width), F32)]
    step_rows = along((once, bands, width), 0)
    full_rows = along((3, once, bands, width), 1)

    def adjoint_first(slots_ref, m0, m1, *refs):
        piece_refs, full_ref, outs, total = refs[:split], refs[split], refs[split + 1 : -1], refs[-1]
        b = lax.axis_index("band")
        for d in range(split):
            at = pl.ds(pl.multiple_of((b ^ d) * part_bands, part_bands), part_bands)
            for a in range(3):
                for q in range(once):
                    full_ref[a, q, at, :] = piece_refs[d][a, :, q * width : (q + 1) * width]

        def value_of(q):
            return ((1.0 - full_ref[0, q]) * full_ref[2, q]).astype(BF16)

        scatter_products(slots_ref, (m0, m1), value_of, outs, total)

    def arrived(refs, q):
        value = refs[0][q]
        for ref in refs[1:]:
            value = value + ref[q].astype(F32)
        return value

    def adjoint_second(slots_ref, m0, m1, *refs):
        got_refs, (full_ref, one_ref), outs, total = (
            refs[: 2 * split],
            refs[2 * split : 2 * split + 2],
            refs[2 * split + 2 : -1],
            refs[-1],
        )

        def value_of(q):
            value = arrived(got_refs, q)
            one_ref[q] = value
            return ((1.0 - full_ref[0, q]) * value).astype(BF16)

        scatter_products(slots_ref, (m0, m1), value_of, outs, total)

    def merge(own_ref, near_ref, kept_ref, *sent_refs):
        kept_ref[...] = own_ref[0] + near_ref[0].astype(F32)
        for d in range(1, split):
            sent_refs[d - 1][...] = (own_ref[d] + near_ref[d].astype(F32)).astype(BF16)

    def collect(own, near, *far):
        near = inner(near)
        far = [outer_across(far[d], d) for d in range(split)]
        kept, *sent = kernel_call(
            merge,
            1,
            0,
            [whole(part_shape)] * 2,
            [(whole(block_shape), shape(block_shape, F32))]
            + [(whole(block_shape), shape(block_shape, BF16))] * (split - 1),
            (own, near),
        )
        return [kept] + [across(sent[d - 1], d) for d in range(1, split)] + far

    def products(slots_ref, m_refs, held, finish):
        i = pl.program_id(0)
        for q in range(once):
            value = jnp.zeros((bands, width), F32)
            for k in range(depth):
                s = slots_ref[(i * once + q) * depth + k]
                value = value + nt(held[s], m_refs[k // half][q, k % half])
            finish(q, value)

    def forward_first(slots_ref, m0, m1, *refs):
        pair_refs, (near_ref, full_ref, zero_ref, rad_ref, held) = refs[:split], refs[split:]
        band = lax.axis_index("band")

        @pl.when(pl.program_id(0) == 0)
        def _():
            def fill(c, carry):
                for third_index in range(3):
                    if third_index == 1:
                        parts = [near_ref[d, c].astype(F32) for d in range(split)]
                    else:
                        parts = [ref[third_index // 2, c].astype(F32) for ref in pair_refs]
                    held[third_index * per_group + c] = jnp.concatenate(parts, axis=0).astype(BF16)
                return carry

            lax.fori_loop(0, per_group, fill, 0)

        def finish(q, value):
            for d in range(split):
                at = pl.ds(pl.multiple_of((band ^ d) * part_bands, part_bands), part_bands)
                zero_ref[q, at, :] = value[d * part_bands : (d + 1) * part_bands]
            e, b = full_ref[0, q], full_ref[1, q]
            rad_ref[q] = (e * b + (1.0 - e) * zero_ref[q]).astype(BF16)

        products(slots_ref, (m0, m1), held, finish)

    def forward_second(slots_ref, m0, m1, *refs):
        pair_refs, (near_ref, full_ref, one_ref, rad_ref, held) = refs[:split], refs[split:]

        @pl.when(pl.program_id(0) == 0)
        def _():
            b = lax.axis_index("band")
            for d in range(split):
                at = (b ^ d) * rb_count
                held[pl.ds(at, rb_count)] = pair_refs[d][0]
                held[pl.ds(per_group + at, rb_count)] = near_ref[d]
                held[pl.ds(2 * per_group + at, rb_count)] = pair_refs[d][1]

        def finish(q, value):
            one_ref[q] = value
            e, b = full_ref[0, q], full_ref[1, q]
            rad_ref[:, q * width : (q + 1) * width] = e * b + (1.0 - e) * value

        products(slots_ref, (m0, m1), held, finish)

    window_scratch = [pltpu.VMEM((3 * per_group, bands, width), BF16)]

    tail = max(0, capacity - LANES)
    seats = LANES + (LANES // 2 if tail else 0)
    value_rows = bands + (bands // 2 if tail else 0)
    send_rows = value_rows + 8

    def route(owner_ref, surface_ref, rank_ref, label_ref):
        names = iota((devices, width), 0)
        upper = (iota((width, width), 0) <= iota((width, width), 1)).astype(BF16)
        seat = iota((seats, width), 0)
        count = jnp.zeros((devices, 1), F32)
        found = jnp.zeros((3 * devices, seats), F32)
        for c in range(rb_count):
            cut = slice(c * width, (c + 1) * width)
            hit = (owner_ref[:, cut] == names).astype(F32)
            rank = nn(hit.astype(BF16), upper) + count
            count = rank[:, width - 1 : width]
            place = jnp.sum(hit * rank, axis=0, keepdims=True).astype(I32) - 1
            rank_ref[:, cut] = place
            seated = (seat == place).astype(F32).astype(BF16)
            surface = surface_ref[:, cut]
            high = (surface >> 7).astype(F32)
            low = (surface & 127).astype(F32)
            marks = jnp.concatenate([hit, hit * high, hit * low], axis=0).astype(BF16)
            found = found + nt(marks, seated)
        taken, high, low = (found[a * devices : (a + 1) * devices] for a in range(3))
        label_ref[...] = jnp.where(taken > 0.5, high * 128.0 + low, float(surfaces))

    rank, labels = kernel_call(
        route,
        1,
        0,
        [whole((1, rows))] * 2,
        [
            (whole((1, rows)), shape((1, rows), I32)),
            (whole((devices, seats)), shape((devices, seats), F32)),
        ],
        (patch_owner.reshape(1, rows), patch_surface.reshape(1, rows)),
    )

    owners_once = 4

    def pack_rows(*refs):
        got_refs = refs[: 2 * split]
        adj_ref, zero_ref, one_ref, full_ref, owner_ref, rank_ref, label_ref = refs[
            2 * split : 2 * split + 7
        ]
        send_ref, grad, digits, seated, most = refs[2 * split + 7 :]
        i = pl.program_id(0)

        @pl.when(i == 0)
        def _():
            most[...] = jnp.full_like(most, 1e-30)

        for q in range(once):
            b, w = full_ref[1, q], full_ref[2, q]
            a = adj_ref[q]
            value = (w + a + arrived(got_refs, q)) * b - (w * one_ref[q] + a * zero_ref[q])
            cut = pl.ds(pl.multiple_of((i * once + q) * width, width), width)
            grad[:, cut] = value
            most[...] = jnp.maximum(most[...], jnp.max(jnp.abs(value), axis=1, keepdims=True))

        @pl.when(i == pl.num_programs(0) - 1)
        def _():
            power = jnp.floor(jnp.log2(most[...])) - 14.0
            power = jnp.where(most[...] * jnp.exp2(-power) > TOP, power + 1.0, power)
            scale = jnp.exp2(-power)[:, :1]
            ordinal = jnp.round(jnp.clip(grad[...] * scale, -TOP, TOP))
            high = ordinal.astype(BF16)
            digits[:bands] = high
            digits[bands:] = (ordinal - high.astype(F32)).astype(BF16)
            seated[...] = (iota((seats, rows), 0) == rank_ref[...]).astype(F32).astype(BF16)
            powers = power.T[:1]
            powers = jnp.concatenate([powers, jnp.zeros((1, LANES - bands), F32)], axis=1)

            def step(c, carry):
                hits = []
                for j in range(owners_once):
                    hit = (owner_ref[...] == c * owners_once + j).astype(F32).astype(BF16)
                    hits.append(digits[...] * hit)
                moved = nt(jnp.concatenate(hits, axis=0), seated[...])
                for j in range(owners_once):
                    at = 2 * bands * j
                    block = moved[at : at + bands] + moved[at + bands : at + 2 * bands]
                    label = label_ref[pl.ds(c * owners_once + j, 1)]
                    parts = [block[:, :LANES]]
                    extra = [label[:, :LANES]]
                    if tail:
                        over = block[:, LANES:]
                        parts.append(
                            jnp.concatenate([over[: bands // 2], over[bands // 2 :]], axis=1)
                        )
                        over = label[:, LANES:]
                        extra.append(jnp.concatenate([over, over], axis=1))
                    else:
                        extra.append(jnp.zeros((1, LANES), F32))
                    extra.append(powers)
                    extra.append(jnp.zeros((5, LANES), F32))
                    out = jnp.concatenate(parts + [jnp.concatenate(extra, axis=0)], axis=0)
                    send_ref[c * owners_once + j] = out.astype(I32).astype(jnp.int16)
                return carry

            lax.fori_loop(0, devices // owners_once, step, 0)

    sources_once = 4
    tops = surfaces // LANES
    lot = sources_once * LANES * (2 if tail else 1)
    top_rows = 2 * bands + 16

    def reduce_rows(got_ref, out_ref, scales, total):
        power = got_ref[:, value_rows + 2].astype(F32)
        scale = jnp.exp2(power).T[:bands]
        for s in range(devices):
            scales[s] = jnp.broadcast_to(scale[:, s : s + 1], (bands, LANES))
        total[...] = jnp.zeros_like(total)
        left = iota((bands // 2, LANES), 1) < LANES // 2
        first_half = iota((1, LANES), 1) < LANES // 2

        def step(c, carry):
            values, labels, once_each = [], [], []
            for j in range(sources_once):
                source = c * sources_once + j
                got = got_ref[source].astype(F32)
                grown = scales[source]
                values.append(got[:bands] * grown)
                labels.append(got[value_rows : value_rows + 1])
                once_each.append(jnp.ones((1, LANES), F32))
                if tail:
                    over = got[bands:value_rows]
                    low = jnp.where(left, over * grown[: bands // 2], 0.0)
                    high = jnp.where(left, 0.0, over * grown[bands // 2 :])
                    values.append(jnp.concatenate([low, high], axis=0))
                    labels.append(got[value_rows + 1 : value_rows + 2])
                    once_each.append(jnp.where(first_half, 1.0, 0.0))
            value = jnp.concatenate(values, axis=1)
            label = jnp.concatenate(labels, axis=1).astype(I32)
            counted = jnp.concatenate(once_each, axis=1)
            high = value.astype(BF16)
            low = (value - high.astype(F32)).astype(BF16)
            counted = jnp.broadcast_to(counted, (16, lot)).astype(BF16)
            both = jnp.concatenate([high, low, counted], axis=0)
            seated = (iota((LANES, lot), 0) == (label & 127)).astype(F32).astype(BF16)
            chosen = [both * (label >> 7 == t).astype(F32).astype(BF16) for t in range(tops)]
            total[...] += nt(jnp.concatenate(chosen, axis=0), seated)
            return carry

        lax.fori_loop(0, devices // sources_once, step, 0)
        for t in range(tops):
            at = t * top_rows
            sums = total[at : at + bands] + total[at + bands : at + 2 * bands]
            count = jnp.maximum(total[at + 2 * bands : at + 2 * bands + 1], 1.0)
            out_ref[:, t * LANES : (t + 1) * LANES] = sums / count

    start = pair_of(start)
    slots, rank, labels, _ = lax.optimization_barrier((slots, rank, labels, start))
    full, *parts = kernel_call(
        adjoint_first,
        4,
        1,
        matrix_specs + [along((3, part_bands, once * width), 2)] * split,
        [(full_rows, shape((3,) + block_shape, F32))] + part_outs,
        (slots, matrix, matrix) + tuple(pieces),
        total_scratch,
        flops=pass_flops,
    )
    starts = gather(start, parts[0])
    got_one = collect(*parts)

    zero, rad = kernel_call(
        forward_first,
        4,
        1,
        matrix_specs + [whole((2,) + start_shape)] * split
        + [whole((split,) + start_shape), full_rows],
        [(step_rows, shape(block_shape, F32)), (step_rows, shape(block_shape, BF16))],
        (slots, matrix, matrix) + tuple(starts) + (full,),
        window_scratch,
        flops=pass_flops,
    )
    rad = pair_of(rad)
    got_one[0], _ = lax.optimization_barrier((got_one[0], rad))
    rad, _ = lax.optimization_barrier((rad, got_one))

    adjoint_one, *parts = kernel_call(
        adjoint_second,
        4,
        1,
        matrix_specs + [step_rows] * (2 * split) + [full_rows],
        [(step_rows, shape(block_shape, F32))] + part_outs,
        (slots, matrix, matrix) + tuple(got_one) + (full,),
        total_scratch,
        flops=pass_flops,
    )
    rads = gather(rad, parts[0])
    got_zero = collect(*parts)

    one, radiosity = kernel_call(
        forward_second,
        4,
        1,
        matrix_specs + [whole((2,) + block_shape)] * split + [whole(part_shape), full_rows],
        [
            (step_rows, shape(block_shape, F32)),
            (along((bands, once * width), 1), shape((bands, rows), F32)),
        ],
        (slots, matrix, matrix) + tuple(rads) + (full,),
        window_scratch,
        flops=pass_flops,
    )

    (send,) = kernel_call(
        pack_rows,
        4,
        0,
        [step_rows] * (2 * split + 3)
        + [full_rows, whole((1, rows)), whole((1, rows)), whole((devices, seats))],
        [
            (
                whole((devices, send_rows, LANES)),
                shape((devices, send_rows, LANES), jnp.int16),
            )
        ],
        (
            *got_zero,
            adjoint_one,
            zero,
            one,
            full,
            patch_owner.reshape(1, rows),
            rank,
            labels,
        ),
        [
            pltpu.VMEM((bands, rows), F32),
            pltpu.VMEM((2 * bands, rows), BF16),
            pltpu.VMEM((seats, rows), BF16),
            pltpu.VMEM((bands, LANES), F32),
        ],
    )
    send = lax.all_to_all(send, ("band", "patch"), 0, 0, tiled=True)
    (surface_grad,) = kernel_call(
        reduce_rows,
        1,
        0,
        [whole((devices, send_rows, LANES))],
        [(whole((bands, surfaces)), shape((bands, surfaces), F32))],
        (send,),
        [
            pltpu.VMEM((devices, bands, LANES), F32),
            pltpu.VMEM((tops * top_rows, LANES), F32),
        ],
    )
    return (radiosity.reshape(bands, 1, 1, rows), surface_grad)


def solution(mesh):
    in_specs = (
        P("band", "patch"),
        P("band", "patch"),
        P("band", "patch"),
        P("patch", "band", None, None, None, None),
        P("patch", "band", None, None),
        P("patch", "band", None, None),
        P("patch", "band", None),
    )
    out_specs = (P(None, "patch", "band", None), P(None, ("band", "patch")))
    return jax.shard_map(body, mesh=mesh, in_specs=in_specs, out_specs=out_specs, check_vma=False)
```

```python
import jax
import jax.numpy as jnp
from jax import lax
from jax.experimental import pallas as pl
from jax.experimental.pallas import tpu as pltpu
from jax.sharding import PartitionSpec as P

F32 = jnp.float32
BF16 = jnp.bfloat16
I32 = jnp.int32
LANES = 128
MIB = 1 << 20
VMEM = pl.BlockSpec(memory_space=pltpu.VMEM)
TOP = 32767.0


def shape(dims, dtype):
    return jax.ShapeDtypeStruct(dims, dtype)


def whole(dims):
    return pl.BlockSpec(dims, lambda i, *_: (0,) * len(dims))


def along(dims, axis):
    return pl.BlockSpec(dims, lambda i, *_: tuple(i if d == axis else 0 for d in range(len(dims))))


def nt(a, b):
    return lax.dot_general(a, b, (((1,), (1,)), ((), ())), preferred_element_type=F32)


def nn(a, b):
    return lax.dot_general(a, b, (((1,), (0,)), ((), ())), preferred_element_type=F32)


def iota(dims, axis):
    return lax.broadcasted_iota(I32, dims, axis)


def kernel_call(kernel, steps, scalars, ins, outs, args, scratch=(), limit=24 * MIB, flops=0):
    return pl.pallas_call(
        kernel,
        out_shape=[o for _, o in outs],
        grid_spec=pltpu.PrefetchScalarGridSpec(
            num_scalar_prefetch=scalars,
            grid=(steps,),
            in_specs=ins,
            out_specs=[s for s, _ in outs],
            scratch_shapes=scratch,
        ),
        compiler_params=pltpu.CompilerParams(vmem_limit_bytes=limit),
        cost_estimate=pl.CostEstimate(flops=flops, bytes_accessed=flops // 32, transcendentals=0),
    )(*args)


def body(
    emissivity, blackbody, loss_weights, view_blocks, column_blocks, patch_owner, patch_surface
):
    split = lax.axis_size("band")
    groups = lax.axis_size("patch")
    devices = split * groups
    part_bands = emissivity.shape[0]
    bands = part_bands * split
    rb_count, depth, width = view_blocks.shape[2:5]
    rows = rb_count * width
    per_group = split * rb_count
    group_bits = per_group.bit_length() - 1
    assert 1 << group_bits == per_group
    capacity = max(2, 3 * rows // devices)
    surfaces = rows // 2

    def inner(block):
        return lax.ppermute(block, "patch", [(i, i ^ 1) for i in range(groups)])

    def outer(block):
        return lax.ppermute(
            block, "patch", [(i, (i + (1 if i % 2 else -1)) % groups) for i in range(groups)]
        )

    def across(block, d):
        return lax.ppermute(block, "band", [(i, i ^ d) for i in range(split)])

    matrix = view_blocks.reshape(rb_count, depth, width, width)
    block_shape = (rb_count, bands, width)
    part_shape = (split,) + block_shape
    pass_flops = 2 * bands * rb_count * depth * width * width
    once = rb_count // 4

    def prepare(e_hbm, b_hbm, w_hbm, start_ref, *refs):
        piece_refs, (e_ref, b_ref, w_ref, loaded) = refs[:split], refs[split:]
        band = lax.axis_index("band")
        loads = [
            pltpu.make_async_copy(source, target, loaded.at[a])
            for a, (source, target) in enumerate(((e_hbm, e_ref), (b_hbm, b_ref), (w_hbm, w_ref)))
        ]
        for load in loads:
            load.start()
        for load in loads:
            load.wait()
        for c in range(per_group):
            cut = slice(c * width, (c + 1) * width)
            start_ref[c] = (e_ref[:, cut] * b_ref[:, cut]).astype(BF16)
        for d in range(split):
            cut = pl.ds(pl.multiple_of((band ^ d) * rows, rows), rows)
            for a, ref in enumerate((e_ref, b_ref, w_ref)):
                piece_refs[d][a] = ref[:, cut]

    piece = (3, part_bands, rows)
    start_shape = (per_group, part_bands, width)
    start, *pieces = kernel_call(
        prepare,
        1,
        0,
        [pl.BlockSpec(memory_space=pltpu.HBM)] * 3,
        [(whole(start_shape), shape(start_shape, BF16))]
        + [(whole(piece), shape(piece, F32))] * split,
        (emissivity, blackbody, loss_weights),
        [pltpu.VMEM(emissivity.shape, F32)] * 3 + [pltpu.SemaphoreType.DMA((3,))],
        limit=60 * MIB,
    )
    pieces = [across(pieces[d], d) if d else pieces[d] for d in range(split)]

    def pair_of(block):
        return jnp.stack([block, outer(block)])

    def gather(pair, after):
        pairs = [pair] + [across(pair, d) for d in range(1, split)]
        pairs, _ = lax.optimization_barrier((pairs, after))
        return pairs + [inner(jnp.stack([p[0] for p in pairs]))]

    def scatter_products(slots_ref, m_ref, value_of, outs, total):
        i = pl.program_id(0)

        @pl.when(i == 0)
        def _():
            total[...] = jnp.zeros_like(total)

        for q in range(once):
            u = value_of(q)
            for k in range(depth):
                s = slots_ref[i * once + q, k]
                total[s] += nn(u, m_ref[i * once + q, k])

        @pl.when(i == pl.num_programs(0) - 1)
        def _():
            own_ref, near_ref, far_ref = outs
            band = lax.axis_index("band")
            for d in range(split):
                at = (band ^ d) * rb_count
                own_ref[d] = total[pl.ds(at, rb_count)]
                near_ref[d] = total[pl.ds(per_group + at, rb_count)].astype(BF16)
                far_ref[d] = total[pl.ds(2 * per_group + at, rb_count)].astype(BF16)

    part_outs = [(whole(part_shape), shape(part_shape, t)) for t in (F32, BF16, BF16)]
    total_scratch = [pltpu.VMEM((3 * per_group, bands, width), F32)]
    step_rows = along((once, bands, width), 0)
    full_rows = along((3, once, bands, width), 1)

    def adjoint_first(slots_ref, m_ref, *refs):
        piece_refs, full_ref, outs, total = refs[:split], refs[split], refs[split + 1 : -1], refs[-1]
        b = lax.axis_index("band")
        for d in range(split):
            at = pl.ds(pl.multiple_of((b ^ d) * part_bands, part_bands), part_bands)
            for a in range(3):
                for q in range(once):
                    full_ref[a, q, at, :] = piece_refs[d][a, :, q * width : (q + 1) * width]

        def value_of(q):
            return ((1.0 - full_ref[0, q]) * full_ref[2, q]).astype(BF16)

        scatter_products(slots_ref, m_ref, value_of, outs, total)

    def arrived(refs, q):
        value = refs[0][q]
        for ref in refs[1:]:
            value = value + ref[q].astype(F32)
        return value

    def adjoint_second(slots_ref, m_ref, *refs):
        got_refs, (full_ref, one_ref), outs, total = (
            refs[:split],
            refs[split : split + 2],
            refs[split + 2 : -1],
            refs[-1],
        )

        def value_of(q):
            value = arrived(got_refs, q)
            one_ref[q] = value
            return ((1.0 - full_ref[0, q]) * value).astype(BF16)

        scatter_products(slots_ref, m_ref, value_of, outs, total)

    def merge(own_ref, near_ref, far_ref, kept_ref, *sent_refs):
        for d in range(split):
            value = own_ref[d] + near_ref[d].astype(F32) + far_ref[d].astype(F32)
            if d:
                sent_refs[d - 1][...] = value.astype(BF16)
            else:
                kept_ref[...] = value

    def collect(own, near, far):
        kept, *sent = kernel_call(
            merge,
            1,
            0,
            [whole(part_shape)] * 3,
            [(whole(block_shape), shape(block_shape, F32))]
            + [(whole(block_shape), shape(block_shape, BF16))] * (split - 1),
            (own, inner(near), outer(far)),
        )
        return [kept] + [across(sent[d - 1], d) for d in range(1, split)]

    def products(slots_ref, m_ref, held, finish):
        i = pl.program_id(0)
        for q in range(once):
            value = jnp.zeros((bands, width), F32)
            for k in range(depth):
                s = slots_ref[i * once + q, k]
                value = value + nt(held[s], m_ref[i * once + q, k])
            finish(q, value)

    def forward_first(slots_ref, m_ref, *refs):
        pair_refs, (near_ref, full_ref, zero_ref, rad_ref, held) = refs[:split], refs[split:]
        band = lax.axis_index("band")

        @pl.when(pl.program_id(0) == 0)
        def _():
            def fill(c, carry):
                for third_index in range(3):
                    if third_index == 1:
                        parts = [near_ref[d, c].astype(F32) for d in range(split)]
                    else:
                        parts = [ref[third_index // 2, c].astype(F32) for ref in pair_refs]
                    held[third_index * per_group + c] = jnp.concatenate(parts, axis=0).astype(BF16)
                return carry

            lax.fori_loop(0, per_group, fill, 0)

        def finish(q, value):
            for d in range(split):
                at = pl.ds(pl.multiple_of((band ^ d) * part_bands, part_bands), part_bands)
                zero_ref[q, at, :] = value[d * part_bands : (d + 1) * part_bands]
            e, b = full_ref[0, q], full_ref[1, q]
            rad_ref[q] = (e * b + (1.0 - e) * zero_ref[q]).astype(BF16)

        products(slots_ref, m_ref, held, finish)

    def forward_second(slots_ref, m_ref, *refs):
        pair_refs, (near_ref, full_ref, one_ref, rad_ref, held) = refs[:split], refs[split:]

        @pl.when(pl.program_id(0) == 0)
        def _():
            b = lax.axis_index("band")
            for d in range(split):
                at = (b ^ d) * rb_count
                held[pl.ds(at, rb_count)] = pair_refs[d][0]
                held[pl.ds(per_group + at, rb_count)] = near_ref[d]
                held[pl.ds(2 * per_group + at, rb_count)] = pair_refs[d][1]

        def finish(q, value):
            one_ref[q] = value
            e, b = full_ref[0, q], full_ref[1, q]
            rad_ref[:, q * width : (q + 1) * width] = e * b + (1.0 - e) * value

        products(slots_ref, m_ref, held, finish)

    window_scratch = [pltpu.VMEM((3 * per_group, bands, width), BF16)]

    tail = max(0, capacity - LANES)
    seats = LANES + (LANES // 2 if tail else 0)
    value_rows = bands + (bands // 2 if tail else 0)
    send_rows = value_rows + 8

    def route(
        matrix_ref, column_ref, owner_ref, surface_ref, m_ref, slot_ref, rank_ref, label_ref, loaded
    ):
        loads = [
            pltpu.make_async_copy(matrix_ref.at[r], m_ref.at[r], loaded.at[r])
            for r in range(rb_count)
        ]
        for load in loads:
            load.start()
        me = lax.axis_index("patch")
        column = column_ref[...]
        group = jnp.right_shift(column, group_bits)
        third = jnp.where(group == me, 0, jnp.where(group == (me ^ 1), 1, 2))
        slot_ref[...] = third * per_group + jnp.bitwise_and(column, per_group - 1)
        names = iota((devices, width), 0)
        upper = (iota((width, width), 0) <= iota((width, width), 1)).astype(BF16)
        seat = iota((seats, width), 0)
        count = jnp.zeros((devices, 1), F32)
        found = jnp.zeros((3 * devices, seats), F32)
        for c in range(rb_count):
            cut = slice(c * width, (c + 1) * width)
            hit = (owner_ref[:, cut] == names).astype(F32)
            rank = nn(hit.astype(BF16), upper) + count
            count = rank[:, width - 1 : width]
            place = jnp.sum(hit * rank, axis=0, keepdims=True).astype(I32) - 1
            rank_ref[:, cut] = place
            seated = (seat == place).astype(F32).astype(BF16)
            surface = surface_ref[:, cut]
            high = (surface >> 7).astype(F32)
            low = (surface & 127).astype(F32)
            marks = jnp.concatenate([hit, hit * high, hit * low], axis=0).astype(BF16)
            found = found + nt(marks, seated)
        taken, high, low = (found[a * devices : (a + 1) * devices] for a in range(3))
        label_ref[...] = jnp.where(taken > 0.5, high * 128.0 + low, float(surfaces))
        for load in loads:
            load.wait()

    matrix, slots, rank, labels = kernel_call(
        route,
        1,
        0,
        [pl.BlockSpec(memory_space=pl.ANY), whole((rb_count, depth))] + [whole((1, rows))] * 2,
        [
            (VMEM, pltpu.VMEM(matrix.shape, BF16)),
            (whole((rb_count, depth)), shape((rb_count, depth), I32)),
            (whole((1, rows)), shape((1, rows), I32)),
            (whole((devices, seats)), shape((devices, seats), F32)),
        ],
        (
            matrix,
            column_blocks.reshape(rb_count, depth),
            patch_owner.reshape(1, rows),
            patch_surface.reshape(1, rows),
        ),
        [pltpu.SemaphoreType.DMA((rb_count,))],
        limit=40 * MIB,
    )

    owners_once = 16

    def pack_rows(*refs):
        got_refs = refs[:split]
        adj_ref, zero_ref, one_ref, full_ref, owner_ref, rank_ref, label_ref = refs[
            split : split + 7
        ]
        send_ref, grad, digits, seated, most = refs[split + 7 :]
        i = pl.program_id(0)

        @pl.when(i == 0)
        def _():
            most[...] = jnp.full_like(most, 1e-30)

        for q in range(once):
            b, w = full_ref[1, q], full_ref[2, q]
            a = adj_ref[q]
            value = (w + a + arrived(got_refs, q)) * b - (w * one_ref[q] + a * zero_ref[q])
            cut = pl.ds(pl.multiple_of((i * once + q) * width, width), width)
            grad[:, cut] = value
            most[...] = jnp.maximum(most[...], jnp.max(jnp.abs(value), axis=1, keepdims=True))

        @pl.when(i == pl.num_programs(0) - 1)
        def _():
            power = jnp.floor(jnp.log2(most[...])) - 14.0
            power = jnp.where(most[...] * jnp.exp2(-power) > TOP, power + 1.0, power)
            scale = jnp.exp2(-power)[:, :1]
            ordinal = jnp.round(jnp.clip(grad[...] * scale, -TOP, TOP))
            high = ordinal.astype(BF16)
            digits[:bands] = high
            digits[bands:] = (ordinal - high.astype(F32)).astype(BF16)
            seated[...] = (iota((seats, rows), 0) == rank_ref[...]).astype(F32).astype(BF16)
            powers = power.T[:1]
            powers = jnp.concatenate([powers, jnp.zeros((1, LANES - bands), F32)], axis=1)

            def step(c, carry):
                hits = []
                for j in range(owners_once):
                    hit = (owner_ref[...] == c * owners_once + j).astype(F32).astype(BF16)
                    hits.append(digits[...] * hit)
                moved = nt(jnp.concatenate(hits, axis=0), seated[...])
                for j in range(owners_once):
                    at = 2 * bands * j
                    block = moved[at : at + bands] + moved[at + bands : at + 2 * bands]
                    label = label_ref[pl.ds(c * owners_once + j, 1)]
                    parts = [block[:, :LANES]]
                    extra = [label[:, :LANES]]
                    if tail:
                        over = block[:, LANES:]
                        parts.append(
                            jnp.concatenate([over[: bands // 2], over[bands // 2 :]], axis=1)
                        )
                        over = label[:, LANES:]
                        extra.append(jnp.concatenate([over, over], axis=1))
                    else:
                        extra.append(jnp.zeros((1, LANES), F32))
                    extra.append(powers)
                    extra.append(jnp.zeros((5, LANES), F32))
                    out = jnp.concatenate(parts + [jnp.concatenate(extra, axis=0)], axis=0)
                    send_ref[c * owners_once + j] = out.astype(I32).astype(jnp.int16)
                return carry

            lax.fori_loop(0, devices // owners_once, step, 0)

    sources_once = 16
    tops = surfaces // LANES
    lot = sources_once * LANES * (2 if tail else 1)
    top_rows = 2 * bands + 16

    def reduce_rows(got_ref, out_ref, scales, total):
        power = got_ref[:, value_rows + 2].astype(F32)
        scale = jnp.exp2(power).T[:bands]
        for s in range(devices):
            scales[s] = jnp.broadcast_to(scale[:, s : s + 1], (bands, LANES))
        total[...] = jnp.zeros_like(total)
        left = iota((bands // 2, LANES), 1) < LANES // 2
        first_half = iota((1, LANES), 1) < LANES // 2

        def step(c, carry):
            values, labels, once_each = [], [], []
            for j in range(sources_once):
                source = c * sources_once + j
                got = got_ref[source].astype(F32)
                grown = scales[source]
                values.append(got[:bands] * grown)
                labels.append(got[value_rows : value_rows + 1])
                once_each.append(jnp.ones((1, LANES), F32))
                if tail:
                    over = got[bands:value_rows]
                    low = jnp.where(left, over * grown[: bands // 2], 0.0)
                    high = jnp.where(left, 0.0, over * grown[bands // 2 :])
                    values.append(jnp.concatenate([low, high], axis=0))
                    labels.append(got[value_rows + 1 : value_rows + 2])
                    once_each.append(jnp.where(first_half, 1.0, 0.0))
            value = jnp.concatenate(values, axis=1)
            label = jnp.concatenate(labels, axis=1).astype(I32)
            counted = jnp.concatenate(once_each, axis=1)
            high = value.astype(BF16)
            low = (value - high.astype(F32)).astype(BF16)
            counted = jnp.broadcast_to(counted, (16, lot)).astype(BF16)
            both = jnp.concatenate([high, low, counted], axis=0)
            seated = (iota((LANES, lot), 0) == (label & 127)).astype(F32).astype(BF16)
            chosen = [both * (label >> 7 == t).astype(F32).astype(BF16) for t in range(tops)]
            total[...] += nt(jnp.concatenate(chosen, axis=0), seated)
            return carry

        lax.fori_loop(0, devices // sources_once, step, 0)
        for t in range(tops):
            at = t * top_rows
            sums = total[at : at + bands] + total[at + bands : at + 2 * bands]
            count = jnp.maximum(total[at + 2 * bands : at + 2 * bands + 1], 1.0)
            out_ref[:, t * LANES : (t + 1) * LANES] = sums / count

    start = jnp.stack(lax.optimization_barrier((start, outer(start), rank, pieces))[:2])
    slots, rank, labels, _ = lax.optimization_barrier((slots, rank, labels, start))
    full, *parts = kernel_call(
        adjoint_first,
        4,
        1,
        [VMEM] + [along((3, part_bands, once * width), 2)] * split,
        [(full_rows, shape((3,) + block_shape, F32))] + part_outs,
        (slots, matrix) + tuple(pieces),
        total_scratch,
        flops=pass_flops,
    )
    starts = gather(start, parts[0])
    got_one = collect(*parts)

    zero, rad = kernel_call(
        forward_first,
        4,
        1,
        [VMEM] + [whole((2,) + start_shape)] * split
        + [whole((split,) + start_shape), full_rows],
        [(step_rows, shape(block_shape, F32)), (step_rows, shape(block_shape, BF16))],
        (slots, matrix) + tuple(starts) + (full,),
        window_scratch,
        flops=pass_flops,
    )
    rad = pair_of(rad)
    got_one[0], _ = lax.optimization_barrier((got_one[0], rad))
    rad, _ = lax.optimization_barrier((rad, got_one))

    adjoint_one, *parts = kernel_call(
        adjoint_second,
        4,
        1,
        [VMEM] + [step_rows] * split + [full_rows],
        [(step_rows, shape(block_shape, F32))] + part_outs,
        (slots, matrix) + tuple(got_one) + (full,),
        total_scratch,
        flops=pass_flops,
    )
    rads = gather(rad, parts[0])
    got_zero = collect(*parts)

    one, radiosity = kernel_call(
        forward_second,
        4,
        1,
        [VMEM] + [whole((2,) + block_shape)] * split + [whole(part_shape), full_rows],
        [
            (step_rows, shape(block_shape, F32)),
            (along((bands, once * width), 1), shape((bands, rows), F32)),
        ],
        (slots, matrix) + tuple(rads) + (full,),
        window_scratch,
        flops=pass_flops,
    )

    (send,) = kernel_call(
        pack_rows,
        4,
        0,
        [step_rows] * (split + 3)
        + [full_rows, whole((1, rows)), whole((1, rows)), whole((devices, seats))],
        [
            (
                whole((devices, send_rows, LANES)),
                shape((devices, send_rows, LANES), jnp.int16),
            )
        ],
        (
            *got_zero,
            adjoint_one,
            zero,
            one,
            full,
            patch_owner.reshape(1, rows),
            rank,
            labels,
        ),
        [
            pltpu.VMEM((bands, rows), F32),
            pltpu.VMEM((2 * bands, rows), BF16),
            pltpu.VMEM((seats, rows), BF16),
            pltpu.VMEM((bands, LANES), F32),
        ],
    )
    send = lax.all_to_all(send, ("band", "patch"), 0, 0, tiled=True)
    (surface_grad,) = kernel_call(
        reduce_rows,
        1,
        0,
        [whole((devices, send_rows, LANES))],
        [(whole((bands, surfaces)), shape((bands, surfaces), F32))],
        (send,),
        [
            pltpu.VMEM((devices, bands, LANES), F32),
            pltpu.VMEM((tops * top_rows, LANES), F32),
        ],
    )
    return (radiosity.reshape(bands, 1, 1, rows), surface_grad)


def solution(mesh):
    in_specs = (
        P("band", "patch"),
        P("band", "patch"),
        P("band", "patch"),
        P("patch", "band", None, None, None, None),
        P("patch", "band", None, None),
        P("patch", "band", None, None),
        P("patch", "band", None),
    )
    out_specs = (P(None, "patch", "band", None), P(None, ("band", "patch")))
    return jax.shard_map(body, mesh=mesh, in_specs=in_specs, out_specs=out_specs, check_vma=False)
```

```python
import jax
import jax.numpy as jnp
from jax import lax
from jax.experimental import pallas as pl
from jax.experimental.pallas import tpu as pltpu
from jax.sharding import PartitionSpec as P

F32 = jnp.float32
BF16 = jnp.bfloat16
I32 = jnp.int32
LANES = 128
MIB = 1 << 20
VMEM = pl.BlockSpec(memory_space=pltpu.VMEM)
TOP = 32767.0
RANGES = ((0.099, 0.901), (0.199, 2.001), (0.499, 1.501))


def coded(value, a):
    low, high = RANGES[a]
    scaled = (value - low) * (65535.0 / (high - low)) - 32768.0
    return jnp.round(jnp.clip(scaled, -32768.0, 32767.0)).astype(jnp.int32).astype(jnp.int16)


def decoded(code, a):
    low, high = RANGES[a]
    return (code.astype(F32) + 32768.0) * ((high - low) / 65535.0) + low


def shape(dims, dtype):
    return jax.ShapeDtypeStruct(dims, dtype)


def whole(dims):
    return pl.BlockSpec(dims, lambda i, *_: (0,) * len(dims))


def along(dims, axis):
    return pl.BlockSpec(dims, lambda i, *_: tuple(i if d == axis else 0 for d in range(len(dims))))


def nt(a, b):
    return lax.dot_general(a, b, (((1,), (1,)), ((), ())), preferred_element_type=F32)


def nn(a, b):
    return lax.dot_general(a, b, (((1,), (0,)), ((), ())), preferred_element_type=F32)


def iota(dims, axis):
    return lax.broadcasted_iota(I32, dims, axis)


def kernel_call(kernel, steps, scalars, ins, outs, args, scratch=(), limit=24 * MIB, flops=0):
    return pl.pallas_call(
        kernel,
        out_shape=[o for _, o in outs],
        grid_spec=pltpu.PrefetchScalarGridSpec(
            num_scalar_prefetch=scalars,
            grid=(steps,),
            in_specs=ins,
            out_specs=[s for s, _ in outs],
            scratch_shapes=scratch,
        ),
        compiler_params=pltpu.CompilerParams(vmem_limit_bytes=limit),
        cost_estimate=pl.CostEstimate(flops=flops, bytes_accessed=flops // 32, transcendentals=0),
    )(*args)


def body(
    emissivity, blackbody, loss_weights, view_blocks, column_blocks, patch_owner, patch_surface
):
    split = lax.axis_size("band")
    groups = lax.axis_size("patch")
    devices = split * groups
    part_bands = emissivity.shape[0]
    bands = part_bands * split
    rb_count, depth, width = view_blocks.shape[2:5]
    rows = rb_count * width
    per_group = split * rb_count
    group_bits = per_group.bit_length() - 1
    assert 1 << group_bits == per_group
    capacity = max(2, 3 * rows // devices)
    surfaces = rows // 2

    def inner(block):
        return lax.ppermute(block, "patch", [(i, i ^ 1) for i in range(groups)])

    def outer(block):
        return lax.ppermute(
            block, "patch", [(i, (i + (1 if i % 2 else -1)) % groups) for i in range(groups)]
        )

    def across(block, d):
        return lax.ppermute(block, "band", [(i, i ^ d) for i in range(split)])

    matrix = view_blocks.reshape(rb_count, depth, width, width)
    block_shape = (rb_count, bands, width)
    part_shape = (split,) + block_shape
    pass_flops = 2 * bands * rb_count * depth * width * width
    once = rb_count // 4

    def prepare(e_hbm, b_hbm, w_hbm, start_ref, *refs):
        piece_refs, (e_ref, b_ref, w_ref, loaded) = refs[:split], refs[split:]
        band = lax.axis_index("band")
        loads = [
            pltpu.make_async_copy(source, target, loaded.at[a])
            for a, (source, target) in enumerate(((e_hbm, e_ref), (b_hbm, b_ref), (w_hbm, w_ref)))
        ]
        for load in loads:
            load.start()
        for load in loads:
            load.wait()
        for c in range(per_group):
            cut = slice(c * width, (c + 1) * width)
            start_ref[c] = (e_ref[:, cut] * b_ref[:, cut]).astype(BF16)
        for d in range(split):
            cut = pl.ds(pl.multiple_of((band ^ d) * rows, rows), rows)
            for a, ref in enumerate((e_ref, b_ref, w_ref)):
                piece_refs[d][a] = coded(ref[:, cut], a)

    piece = (3, part_bands, rows)
    start_shape = (per_group, part_bands, width)
    start, *pieces = kernel_call(
        prepare,
        1,
        0,
        [pl.BlockSpec(memory_space=pltpu.HBM)] * 3,
        [(whole(start_shape), shape(start_shape, BF16))]
        + [(whole(piece), shape(piece, jnp.int16))] * split,
        (emissivity, blackbody, loss_weights),
        [pltpu.VMEM(emissivity.shape, F32)] * 3 + [pltpu.SemaphoreType.DMA((3,))],
        limit=60 * MIB,
    )
    pieces = [across(pieces[d], d) if d else pieces[d] for d in range(split)]

    def pair_of(block):
        return jnp.stack([block, outer(block)])

    def gather(pair, after):
        pairs = [pair] + [across(pair, d) for d in range(1, split)]
        pairs, _ = lax.optimization_barrier((pairs, after))
        return pairs + [inner(jnp.stack([p[0] for p in pairs]))]

    def scatter_products(slots_ref, m_ref, value_of, outs, total):
        i = pl.program_id(0)

        @pl.when(i == 0)
        def _():
            total[...] = jnp.zeros_like(total)

        for q in range(once):
            u = value_of(q)
            for k in range(depth):
                s = slots_ref[i * once + q, k]
                total[s] += nn(u, m_ref[i * once + q, k])

        @pl.when(i == pl.num_programs(0) - 1)
        def _():
            own_ref, near_ref, far_ref = outs
            band = lax.axis_index("band")
            for d in range(split):
                at = (band ^ d) * rb_count
                own_ref[d] = total[pl.ds(at, rb_count)]
                near_ref[d] = total[pl.ds(per_group + at, rb_count)].astype(BF16)
                far_ref[d] = total[pl.ds(2 * per_group + at, rb_count)].astype(BF16)

    part_outs = [(whole(part_shape), shape(part_shape, t)) for t in (F32, BF16, BF16)]
    total_scratch = [pltpu.VMEM((3 * per_group, bands, width), F32)]
    step_rows = along((once, bands, width), 0)
    full_rows = along((3, once, bands, width), 1)

    def adjoint_first(slots_ref, m_ref, *refs):
        piece_refs, full_ref, outs, total = refs[:split], refs[split], refs[split + 1 : -1], refs[-1]
        b = lax.axis_index("band")
        for d in range(split):
            at = pl.ds(pl.multiple_of((b ^ d) * part_bands, part_bands), part_bands)
            for a in range(3):
                for q in range(once):
                    code = piece_refs[d][a, :, q * width : (q + 1) * width]
                    full_ref[a, q, at, :] = decoded(code, a)

        def value_of(q):
            return ((1.0 - full_ref[0, q]) * full_ref[2, q]).astype(BF16)

        scatter_products(slots_ref, m_ref, value_of, outs, total)

    def arrived(refs, q):
        value = refs[0][q]
        for ref in refs[1:]:
            value = value + ref[q].astype(F32)
        return value

    def adjoint_second(slots_ref, m_ref, *refs):
        got_refs, (full_ref, one_ref), outs, total = (
            refs[:split],
            refs[split : split + 2],
            refs[split + 2 : -1],
            refs[-1],
        )

        def value_of(q):
            value = arrived(got_refs, q)
            one_ref[q] = value
            return ((1.0 - full_ref[0, q]) * value).astype(BF16)

        scatter_products(slots_ref, m_ref, value_of, outs, total)

    def merge(own_ref, near_ref, far_ref, kept_ref, *sent_refs):
        for d in range(split):
            value = own_ref[d] + near_ref[d].astype(F32) + far_ref[d].astype(F32)
            if d:
                sent_refs[d - 1][...] = value.astype(BF16)
            else:
                kept_ref[...] = value

    def collect(own, near, far):
        kept, *sent = kernel_call(
            merge,
            1,
            0,
            [whole(part_shape)] * 3,
            [(whole(block_shape), shape(block_shape, F32))]
            + [(whole(block_shape), shape(block_shape, BF16))] * (split - 1),
            (own, inner(near), outer(far)),
        )
        return [kept] + [across(sent[d - 1], d) for d in range(1, split)]

    def products(slots_ref, m_ref, held, finish):
        i = pl.program_id(0)
        for q in range(once):
            value = jnp.zeros((bands, width), F32)
            for k in range(depth):
                s = slots_ref[i * once + q, k]
                value = value + nt(held[s], m_ref[i * once + q, k])
            finish(q, value)

    def forward_first(slots_ref, m_ref, *refs):
        pair_refs, (near_ref, full_ref, zero_ref, rad_ref, held) = refs[:split], refs[split:]
        band = lax.axis_index("band")

        @pl.when(pl.program_id(0) == 0)
        def _():
            def fill(c, carry):
                for third_index in range(3):
                    if third_index == 1:
                        parts = [near_ref[d, c].astype(F32) for d in range(split)]
                    else:
                        parts = [ref[third_index // 2, c].astype(F32) for ref in pair_refs]
                    held[third_index * per_group + c] = jnp.concatenate(parts, axis=0).astype(BF16)
                return carry

            lax.fori_loop(0, per_group, fill, 0)

        def finish(q, value):
            for d in range(split):
                at = pl.ds(pl.multiple_of((band ^ d) * part_bands, part_bands), part_bands)
                zero_ref[q, at, :] = value[d * part_bands : (d + 1) * part_bands]
            e, b = full_ref[0, q], full_ref[1, q]
            rad_ref[q] = (e * b + (1.0 - e) * zero_ref[q]).astype(BF16)

        products(slots_ref, m_ref, held, finish)

    def forward_second(slots_ref, m_ref, *refs):
        pair_refs, (near_ref, full_ref, one_ref, rad_ref, held) = refs[:split], refs[split:]

        @pl.when(pl.program_id(0) == 0)
        def _():
            b = lax.axis_index("band")
            for d in range(split):
                at = (b ^ d) * rb_count
                held[pl.ds(at, rb_count)] = pair_refs[d][0]
                held[pl.ds(per_group + at, rb_count)] = near_ref[d]
                held[pl.ds(2 * per_group + at, rb_count)] = pair_refs[d][1]

        def finish(q, value):
            one_ref[q] = value
            e, b = full_ref[0, q], full_ref[1, q]
            rad_ref[:, q * width : (q + 1) * width] = e * b + (1.0 - e) * value

        products(slots_ref, m_ref, held, finish)

    window_scratch = [pltpu.VMEM((3 * per_group, bands, width), BF16)]

    tail = max(0, capacity - LANES)
    seats = LANES + (LANES // 2 if tail else 0)
    value_rows = bands + (bands // 2 if tail else 0)
    send_rows = value_rows + 8

    def route(
        matrix_ref, column_ref, owner_ref, surface_ref, m_ref, slot_ref, rank_ref, label_ref, loaded
    ):
        loads = [
            pltpu.make_async_copy(matrix_ref.at[r], m_ref.at[r], loaded.at[r])
            for r in range(rb_count)
        ]
        for load in loads:
            load.start()
        me = lax.axis_index("patch")
        column = column_ref[...]
        group = jnp.right_shift(column, group_bits)
        third = jnp.where(group == me, 0, jnp.where(group == (me ^ 1), 1, 2))
        slot_ref[...] = third * per_group + jnp.bitwise_and(column, per_group - 1)
        names = iota((devices, width), 0)
        upper = (iota((width, width), 0) <= iota((width, width), 1)).astype(BF16)
        seat = iota((seats, width), 0)
        count = jnp.zeros((devices, 1), F32)
        found = jnp.zeros((3 * devices, seats), F32)
        for c in range(rb_count):
            cut = slice(c * width, (c + 1) * width)
            hit = (owner_ref[:, cut] == names).astype(F32)
            rank = nn(hit.astype(BF16), upper) + count
            count = rank[:, width - 1 : width]
            place = jnp.sum(hit * rank, axis=0, keepdims=True).astype(I32) - 1
            rank_ref[:, cut] = place
            seated = (seat == place).astype(F32).astype(BF16)
            surface = surface_ref[:, cut]
            high = (surface >> 7).astype(F32)
            low = (surface & 127).astype(F32)
            marks = jnp.concatenate([hit, hit * high, hit * low], axis=0).astype(BF16)
            found = found + nt(marks, seated)
        taken, high, low = (found[a * devices : (a + 1) * devices] for a in range(3))
        label_ref[...] = jnp.where(taken > 0.5, high * 128.0 + low, float(surfaces))
        for load in loads:
            load.wait()

    matrix, slots, rank, labels = kernel_call(
        route,
        1,
        0,
        [pl.BlockSpec(memory_space=pl.ANY), whole((rb_count, depth))] + [whole((1, rows))] * 2,
        [
            (VMEM, pltpu.VMEM(matrix.shape, BF16)),
            (whole((rb_count, depth)), shape((rb_count, depth), I32)),
            (whole((1, rows)), shape((1, rows), I32)),
            (whole((devices, seats)), shape((devices, seats), F32)),
        ],
        (
            matrix,
            column_blocks.reshape(rb_count, depth),
            patch_owner.reshape(1, rows),
            patch_surface.reshape(1, rows),
        ),
        [pltpu.SemaphoreType.DMA((rb_count,))],
        limit=40 * MIB,
    )

    owners_once = 32

    def pack_rows(*refs):
        got_refs = refs[:split]
        adj_ref, zero_ref, one_ref, full_ref, owner_ref, rank_ref, label_ref = refs[
            split : split + 7
        ]
        send_ref, grad, digits, seated, most = refs[split + 7 :]
        i = pl.program_id(0)

        @pl.when(i == 0)
        def _():
            most[...] = jnp.full_like(most, 1e-30)

        for q in range(once):
            b, w = full_ref[1, q], full_ref[2, q]
            a = adj_ref[q]
            value = (w + a + arrived(got_refs, q)) * b - (w * one_ref[q] + a * zero_ref[q])
            cut = pl.ds(pl.multiple_of((i * once + q) * width, width), width)
            grad[:, cut] = value
            most[...] = jnp.maximum(most[...], jnp.max(jnp.abs(value), axis=1, keepdims=True))

        @pl.when(i == pl.num_programs(0) - 1)
        def _():
            power = jnp.floor(jnp.log2(most[...])) - 14.0
            power = jnp.where(most[...] * jnp.exp2(-power) > TOP, power + 1.0, power)
            scale = jnp.exp2(-power)[:, :1]
            ordinal = jnp.round(jnp.clip(grad[...] * scale, -TOP, TOP))
            high = ordinal.astype(BF16)
            digits[:bands] = high
            digits[bands:] = (ordinal - high.astype(F32)).astype(BF16)
            seated[...] = (iota((seats, rows), 0) == rank_ref[...]).astype(F32).astype(BF16)
            powers = power.T[:1]
            powers = jnp.concatenate([powers, jnp.zeros((1, LANES - bands), F32)], axis=1)

            def step(c, carry):
                hits = []
                for j in range(owners_once):
                    hit = (owner_ref[...] == c * owners_once + j).astype(F32).astype(BF16)
                    hits.append(digits[...] * hit)
                moved = nt(jnp.concatenate(hits, axis=0), seated[...])
                for j in range(owners_once):
                    at = 2 * bands * j
                    block = moved[at : at + bands] + moved[at + bands : at + 2 * bands]
                    label = label_ref[pl.ds(c * owners_once + j, 1)]
                    parts = [block[:, :LANES]]
                    extra = [label[:, :LANES]]
                    if tail:
                        over = block[:, LANES:]
                        parts.append(
                            jnp.concatenate([over[: bands // 2], over[bands // 2 :]], axis=1)
                        )
                        over = label[:, LANES:]
                        extra.append(jnp.concatenate([over, over], axis=1))
                    else:
                        extra.append(jnp.zeros((1, LANES), F32))
                    extra.append(powers)
                    extra.append(jnp.zeros((5, LANES), F32))
                    out = jnp.concatenate(parts + [jnp.concatenate(extra, axis=0)], axis=0)
                    send_ref[c * owners_once + j] = out.astype(I32).astype(jnp.int16)
                return carry

            lax.fori_loop(0, devices // owners_once, step, 0)

    sources_once = 32
    tops = surfaces // LANES
    lot = sources_once * LANES * (2 if tail else 1)
    top_rows = 2 * bands + 16

    def reduce_rows(got_ref, out_ref, scales, total):
        power = got_ref[:, value_rows + 2].astype(F32)
        scale = jnp.exp2(power).T[:bands]
        for s in range(devices):
            scales[s] = jnp.broadcast_to(scale[:, s : s + 1], (bands, LANES))
        total[...] = jnp.zeros_like(total)
        left = iota((bands // 2, LANES), 1) < LANES // 2
        first_half = iota((1, LANES), 1) < LANES // 2

        def step(c, carry):
            values, labels, once_each = [], [], []
            for j in range(sources_once):
                source = c * sources_once + j
                got = got_ref[source].astype(F32)
                grown = scales[source]
                values.append(got[:bands] * grown)
                labels.append(got[value_rows : value_rows + 1])
                once_each.append(jnp.ones((1, LANES), F32))
                if tail:
                    over = got[bands:value_rows]
                    low = jnp.where(left, over * grown[: bands // 2], 0.0)
                    high = jnp.where(left, 0.0, over * grown[bands // 2 :])
                    values.append(jnp.concatenate([low, high], axis=0))
                    labels.append(got[value_rows + 1 : value_rows + 2])
                    once_each.append(jnp.where(first_half, 1.0, 0.0))
            value = jnp.concatenate(values, axis=1)
            label = jnp.concatenate(labels, axis=1).astype(I32)
            counted = jnp.concatenate(once_each, axis=1)
            high = value.astype(BF16)
            low = (value - high.astype(F32)).astype(BF16)
            counted = jnp.broadcast_to(counted, (16, lot)).astype(BF16)
            both = jnp.concatenate([high, low, counted], axis=0)
            seated = (iota((LANES, lot), 0) == (label & 127)).astype(F32).astype(BF16)
            chosen = [both * (label >> 7 == t).astype(F32).astype(BF16) for t in range(tops)]
            total[...] += nt(jnp.concatenate(chosen, axis=0), seated)
            return carry

        lax.fori_loop(0, devices // sources_once, step, 0)
        for t in range(tops):
            at = t * top_rows
            sums = total[at : at + bands] + total[at + bands : at + 2 * bands]
            count = jnp.maximum(total[at + 2 * bands : at + 2 * bands + 1], 1.0)
            out_ref[:, t * LANES : (t + 1) * LANES] = sums / count

    start = jnp.stack(lax.optimization_barrier((start, outer(start), rank, pieces))[:2])
    slots, rank, labels, _ = lax.optimization_barrier((slots, rank, labels, start))
    full, *parts = kernel_call(
        adjoint_first,
        4,
        1,
        [VMEM] + [along((3, part_bands, once * width), 2)] * split,
        [(full_rows, shape((3,) + block_shape, F32))] + part_outs,
        (slots, matrix) + tuple(pieces),
        total_scratch,
        flops=pass_flops,
    )
    starts = gather(start, parts[0])
    got_one = collect(*parts)

    zero, rad = kernel_call(
        forward_first,
        4,
        1,
        [VMEM] + [whole((2,) + start_shape)] * split
        + [whole((split,) + start_shape), full_rows],
        [(step_rows, shape(block_shape, F32)), (step_rows, shape(block_shape, BF16))],
        (slots, matrix) + tuple(starts) + (full,),
        window_scratch,
        flops=pass_flops,
    )
    rad = pair_of(rad)
    got_one[0], _ = lax.optimization_barrier((got_one[0], rad))
    rad, _ = lax.optimization_barrier((rad, got_one))

    adjoint_one, *parts = kernel_call(
        adjoint_second,
        4,
        1,
        [VMEM] + [step_rows] * split + [full_rows],
        [(step_rows, shape(block_shape, F32))] + part_outs,
        (slots, matrix) + tuple(got_one) + (full,),
        total_scratch,
        flops=pass_flops,
    )
    rads = gather(rad, parts[0])
    got_zero = collect(*parts)

    one, radiosity = kernel_call(
        forward_second,
        4,
        1,
        [VMEM] + [whole((2,) + block_shape)] * split + [whole(part_shape), full_rows],
        [
            (step_rows, shape(block_shape, F32)),
            (along((bands, once * width), 1), shape((bands, rows), F32)),
        ],
        (slots, matrix) + tuple(rads) + (full,),
        window_scratch,
        flops=pass_flops,
    )

    (send,) = kernel_call(
        pack_rows,
        4,
        0,
        [step_rows] * (split + 3)
        + [full_rows, whole((1, rows)), whole((1, rows)), whole((devices, seats))],
        [
            (
                whole((devices, send_rows, LANES)),
                shape((devices, send_rows, LANES), jnp.int16),
            )
        ],
        (
            *got_zero,
            adjoint_one,
            zero,
            one,
            full,
            patch_owner.reshape(1, rows),
            rank,
            labels,
        ),
        [
            pltpu.VMEM((bands, rows), F32),
            pltpu.VMEM((2 * bands, rows), BF16),
            pltpu.VMEM((seats, rows), BF16),
            pltpu.VMEM((bands, LANES), F32),
        ],
    )
    send = lax.all_to_all(send, ("band", "patch"), 0, 0, tiled=True)
    (surface_grad,) = kernel_call(
        reduce_rows,
        1,
        0,
        [whole((devices, send_rows, LANES))],
        [(whole((bands, surfaces)), shape((bands, surfaces), F32))],
        (send,),
        [
            pltpu.VMEM((devices, bands, LANES), F32),
            pltpu.VMEM((tops * top_rows, LANES), F32),
        ],
    )
    return (radiosity.reshape(bands, 1, 1, rows), surface_grad)


def solution(mesh):
    in_specs = (
        P("band", "patch"),
        P("band", "patch"),
        P("band", "patch"),
        P("patch", "band", None, None, None, None),
        P("patch", "band", None, None),
        P("patch", "band", None, None),
        P("patch", "band", None),
    )
    out_specs = (P(None, "patch", "band", None), P(None, ("band", "patch")))
    return jax.shard_map(body, mesh=mesh, in_specs=in_specs, out_specs=out_specs, check_vma=False)
```

```python
import jax
import jax.numpy as jnp
from jax import lax
from jax.experimental import pallas as pl
from jax.experimental.pallas import tpu as pltpu
from jax.sharding import PartitionSpec as P

F32 = jnp.float32
BF16 = jnp.bfloat16
I32 = jnp.int32
LANES = 128
MIB = 1 << 20
VMEM = pl.BlockSpec(memory_space=pltpu.VMEM)
TOP = 32767.0
RANGES = ((0.099, 0.901), (0.199, 2.001), (0.499, 1.501))


def coded(value, a):
    low, high = RANGES[a]
    scaled = (value - low) * (65535.0 / (high - low)) - 32768.0
    return jnp.round(jnp.clip(scaled, -32768.0, 32767.0)).astype(jnp.int32).astype(jnp.int16)


def decoded(code, a):
    low, high = RANGES[a]
    return (code.astype(F32) + 32768.0) * ((high - low) / 65535.0) + low


def shape(dims, dtype):
    return jax.ShapeDtypeStruct(dims, dtype)


def whole(dims):
    return pl.BlockSpec(dims, lambda i, *_: (0,) * len(dims))


def along(dims, axis):
    return pl.BlockSpec(dims, lambda i, *_: tuple(i if d == axis else 0 for d in range(len(dims))))


def nt(a, b):
    return lax.dot_general(a, b, (((1,), (1,)), ((), ())), preferred_element_type=F32)


def nn(a, b):
    return lax.dot_general(a, b, (((1,), (0,)), ((), ())), preferred_element_type=F32)


def iota(dims, axis):
    return lax.broadcasted_iota(I32, dims, axis)


def kernel_call(kernel, steps, scalars, ins, outs, args, scratch=(), limit=24 * MIB, flops=0):
    return pl.pallas_call(
        kernel,
        out_shape=[o for _, o in outs],
        grid_spec=pltpu.PrefetchScalarGridSpec(
            num_scalar_prefetch=scalars,
            grid=(steps,),
            in_specs=ins,
            out_specs=[s for s, _ in outs],
            scratch_shapes=scratch,
        ),
        compiler_params=pltpu.CompilerParams(vmem_limit_bytes=limit),
        cost_estimate=pl.CostEstimate(flops=flops, bytes_accessed=flops // 32, transcendentals=0),
    )(*args)


def body(
    emissivity, blackbody, loss_weights, view_blocks, column_blocks, patch_owner, patch_surface
):
    split = lax.axis_size("band")
    groups = lax.axis_size("patch")
    devices = split * groups
    part_bands = emissivity.shape[0]
    bands = part_bands * split
    rb_count, depth, width = view_blocks.shape[2:5]
    rows = rb_count * width
    per_group = split * rb_count
    group_bits = per_group.bit_length() - 1
    assert 1 << group_bits == per_group
    capacity = max(2, 3 * rows // devices)
    surfaces = rows // 2

    def inner(block):
        return lax.ppermute(block, "patch", [(i, i ^ 1) for i in range(groups)])

    def outer(block):
        return lax.ppermute(
            block, "patch", [(i, (i + (1 if i % 2 else -1)) % groups) for i in range(groups)]
        )

    def across(block, d):
        return lax.ppermute(block, "band", [(i, i ^ d) for i in range(split)])

    matrix = view_blocks.reshape(rb_count, depth, width, width)
    block_shape = (rb_count, bands, width)
    part_shape = (split,) + block_shape
    pass_flops = 2 * bands * rb_count * depth * width * width
    once = rb_count // 4

    def prepare(e_hbm, b_hbm, w_hbm, start_ref, *refs):
        piece_refs, (e_ref, b_ref, w_ref, loaded) = refs[:split], refs[split:]
        band = lax.axis_index("band")
        loads = [
            pltpu.make_async_copy(source, target, loaded.at[a])
            for a, (source, target) in enumerate(((e_hbm, e_ref), (b_hbm, b_ref), (w_hbm, w_ref)))
        ]
        for load in loads:
            load.start()
        for load in loads:
            load.wait()
        for c in range(per_group):
            cut = slice(c * width, (c + 1) * width)
            start_ref[c] = (e_ref[:, cut] * b_ref[:, cut]).astype(BF16)
        for d in range(split):
            cut = pl.ds(pl.multiple_of((band ^ d) * rows, rows), rows)
            for a, ref in enumerate((e_ref, b_ref, w_ref)):
                piece_refs[d][a] = coded(ref[:, cut], a)

    piece = (3, part_bands, rows)
    start_shape = (per_group, part_bands, width)
    start, *pieces = kernel_call(
        prepare,
        1,
        0,
        [pl.BlockSpec(memory_space=pltpu.HBM)] * 3,
        [(whole(start_shape), shape(start_shape, BF16))]
        + [(whole(piece), shape(piece, jnp.int16))] * split,
        (emissivity, blackbody, loss_weights),
        [pltpu.VMEM(emissivity.shape, F32)] * 3 + [pltpu.SemaphoreType.DMA((3,))],
        limit=60 * MIB,
    )
    pieces = [across(pieces[d], d) if d else pieces[d] for d in range(split)]

    def pair_of(block):
        return jnp.stack([block, outer(block)])

    def gather(pair, after):
        pairs = [pair] + [across(pair, d) for d in range(1, split)]
        pairs, _ = lax.optimization_barrier((pairs, after))
        return pairs + [inner(jnp.stack([p[0] for p in pairs]))]

    def scatter_products(slots_ref, m_ref, value_of, outs, total):
        i = pl.program_id(0)

        @pl.when(i == 0)
        def _():
            total[...] = jnp.zeros_like(total)

        for q in range(once):
            u = value_of(q)
            for k in range(depth):
                s = slots_ref[i * once + q, k]
                total[s] += nn(u, m_ref[i * once + q, k])

        @pl.when(i == pl.num_programs(0) - 1)
        def _():
            own_ref, near_ref, far_ref = outs
            band = lax.axis_index("band")
            for d in range(split):
                at = (band ^ d) * rb_count
                own_ref[d] = total[pl.ds(at, rb_count)]
                near_ref[d] = total[pl.ds(per_group + at, rb_count)].astype(BF16)
                far_ref[d] = total[pl.ds(2 * per_group + at, rb_count)].astype(BF16)

    part_outs = [(whole(part_shape), shape(part_shape, t)) for t in (F32, BF16, BF16)]
    total_scratch = [pltpu.VMEM((3 * per_group, bands, width), F32)]
    step_rows = along((once, bands, width), 0)
    full_rows = along((3, once, bands, width), 1)

    def adjoint_first(slots_ref, matrix_ref, *refs):
        piece_refs, (full_ref, m_ref), outs = refs[:split], refs[split : split + 2], refs[split + 2 : -2]
        total, arrivals = refs[-2:]
        i = pl.program_id(0)

        def copy_of(r):
            return pltpu.make_async_copy(matrix_ref.at[r], m_ref.at[r], arrivals.at[r])

        @pl.when(i == 0)
        def _():
            for r in range(rb_count):
                copy_of(r).start()

        b = lax.axis_index("band")
        for d in range(split):
            at = pl.ds(pl.multiple_of((b ^ d) * part_bands, part_bands), part_bands)
            for a in range(3):
                for q in range(once):
                    code = piece_refs[d][a, :, q * width : (q + 1) * width]
                    full_ref[a, q, at, :] = decoded(code, a)

        def value_of(q):
            copy_of(i * once + q).wait()
            return ((1.0 - full_ref[0, q]) * full_ref[2, q]).astype(BF16)

        scatter_products(slots_ref, m_ref, value_of, outs, total)

    def arrived(refs, q):
        value = refs[0][q]
        for ref in refs[1:]:
            value = value + ref[q].astype(F32)
        return value

    def adjoint_second(slots_ref, m_ref, *refs):
        got_refs, (full_ref, one_ref), outs, total = (
            refs[:split],
            refs[split : split + 2],
            refs[split + 2 : -1],
            refs[-1],
        )

        def value_of(q):
            value = arrived(got_refs, q)
            one_ref[q] = value
            return ((1.0 - full_ref[0, q]) * value).astype(BF16)

        scatter_products(slots_ref, m_ref, value_of, outs, total)

    def merge(own_ref, near_ref, far_ref, kept_ref, *sent_refs):
        for d in range(split):
            value = own_ref[d] + near_ref[d].astype(F32) + far_ref[d].astype(F32)
            if d:
                sent_refs[d - 1][...] = value.astype(BF16)
            else:
                kept_ref[...] = value

    def collect(own, near, far):
        kept, *sent = kernel_call(
            merge,
            1,
            0,
            [whole(part_shape)] * 3,
            [(whole(block_shape), shape(block_shape, F32))]
            + [(whole(block_shape), shape(block_shape, BF16))] * (split - 1),
            (own, inner(near), outer(far)),
        )
        return [kept] + [across(sent[d - 1], d) for d in range(1, split)]

    def products(slots_ref, m_ref, held, finish):
        i = pl.program_id(0)
        for q in range(once):
            value = jnp.zeros((bands, width), F32)
            for k in range(depth):
                s = slots_ref[i * once + q, k]
                value = value + nt(held[s], m_ref[i * once + q, k])
            finish(q, value)

    def forward_first(slots_ref, m_ref, *refs):
        pair_refs, (near_ref, full_ref, zero_ref, rad_ref, held) = refs[:split], refs[split:]
        band = lax.axis_index("band")

        @pl.when(pl.program_id(0) == 0)
        def _():
            def fill(c, carry):
                for third_index in range(3):
                    if third_index == 1:
                        parts = [near_ref[d, c].astype(F32) for d in range(split)]
                    else:
                        parts = [ref[third_index // 2, c].astype(F32) for ref in pair_refs]
                    held[third_index * per_group + c] = jnp.concatenate(parts, axis=0).astype(BF16)
                return carry

            lax.fori_loop(0, per_group, fill, 0)

        def finish(q, value):
            for d in range(split):
                at = pl.ds(pl.multiple_of((band ^ d) * part_bands, part_bands), part_bands)
                zero_ref[q, at, :] = value[d * part_bands : (d + 1) * part_bands]
            e, b = full_ref[0, q], full_ref[1, q]
            rad_ref[q] = (e * b + (1.0 - e) * zero_ref[q]).astype(BF16)

        products(slots_ref, m_ref, held, finish)

    def forward_second(slots_ref, m_ref, *refs):
        pair_refs, (near_ref, full_ref, one_ref, rad_ref, held) = refs[:split], refs[split:]

        @pl.when(pl.program_id(0) == 0)
        def _():
            b = lax.axis_index("band")
            for d in range(split):
                at = (b ^ d) * rb_count
                held[pl.ds(at, rb_count)] = pair_refs[d][0]
                held[pl.ds(per_group + at, rb_count)] = near_ref[d]
                held[pl.ds(2 * per_group + at, rb_count)] = pair_refs[d][1]

        def finish(q, value):
            one_ref[q] = value
            e, b = full_ref[0, q], full_ref[1, q]
            rad_ref[:, q * width : (q + 1) * width] = e * b + (1.0 - e) * value

        products(slots_ref, m_ref, held, finish)

    window_scratch = [pltpu.VMEM((3 * per_group, bands, width), BF16)]

    tail = max(0, capacity - LANES)
    seats = LANES + (LANES // 2 if tail else 0)
    value_rows = bands + (bands // 2 if tail else 0)
    send_rows = value_rows + 8

    def route(column_ref, owner_ref, surface_ref, slot_ref, rank_ref, label_ref):
        me = lax.axis_index("patch")
        column = column_ref[...]
        group = jnp.right_shift(column, group_bits)
        third = jnp.where(group == me, 0, jnp.where(group == (me ^ 1), 1, 2))
        slot_ref[...] = third * per_group + jnp.bitwise_and(column, per_group - 1)
        names = iota((devices, width), 0)
        upper = (iota((width, width), 0) <= iota((width, width), 1)).astype(BF16)
        seat = iota((seats, width), 0)
        count = jnp.zeros((devices, 1), F32)
        found = jnp.zeros((3 * devices, seats), F32)
        for c in range(rb_count):
            cut = slice(c * width, (c + 1) * width)
            hit = (owner_ref[:, cut] == names).astype(F32)
            rank = nn(hit.astype(BF16), upper) + count
            count = rank[:, width - 1 : width]
            place = jnp.sum(hit * rank, axis=0, keepdims=True).astype(I32) - 1
            rank_ref[:, cut] = place
            seated = (seat == place).astype(F32).astype(BF16)
            surface = surface_ref[:, cut]
            high = (surface >> 7).astype(F32)
            low = (surface & 127).astype(F32)
            marks = jnp.concatenate([hit, hit * high, hit * low], axis=0).astype(BF16)
            found = found + nt(marks, seated)
        taken, high, low = (found[a * devices : (a + 1) * devices] for a in range(3))
        label_ref[...] = jnp.where(taken > 0.5, high * 128.0 + low, float(surfaces))

    slots, rank, labels = kernel_call(
        route,
        1,
        0,
        [whole((rb_count, depth))] + [whole((1, rows))] * 2,
        [
            (whole((rb_count, depth)), shape((rb_count, depth), I32)),
            (whole((1, rows)), shape((1, rows), I32)),
            (whole((devices, seats)), shape((devices, seats), F32)),
        ],
        (
            column_blocks.reshape(rb_count, depth),
            patch_owner.reshape(1, rows),
            patch_surface.reshape(1, rows),
        ),
        limit=60 * MIB,
    )

    owners_once = 32

    def pack_rows(*refs):
        got_refs = refs[:split]
        adj_ref, zero_ref, one_ref, full_ref, owner_ref, rank_ref, label_ref = refs[
            split : split + 7
        ]
        send_ref, grad, digits, seated, most = refs[split + 7 :]
        i = pl.program_id(0)

        @pl.when(i == 0)
        def _():
            most[...] = jnp.full_like(most, 1e-30)

        for q in range(once):
            b, w = full_ref[1, q], full_ref[2, q]
            a = adj_ref[q]
            value = (w + a + arrived(got_refs, q)) * b - (w * one_ref[q] + a * zero_ref[q])
            cut = pl.ds(pl.multiple_of((i * once + q) * width, width), width)
            grad[:, cut] = value
            most[...] = jnp.maximum(most[...], jnp.max(jnp.abs(value), axis=1, keepdims=True))

        @pl.when(i == pl.num_programs(0) - 1)
        def _():
            power = jnp.floor(jnp.log2(most[...])) - 14.0
            power = jnp.where(most[...] * jnp.exp2(-power) > TOP, power + 1.0, power)
            scale = jnp.exp2(-power)[:, :1]
            ordinal = jnp.round(jnp.clip(grad[...] * scale, -TOP, TOP))
            high = ordinal.astype(BF16)
            digits[:bands] = high
            digits[bands:] = (ordinal - high.astype(F32)).astype(BF16)
            seated[...] = (iota((seats, rows), 0) == rank_ref[...]).astype(F32).astype(BF16)
            powers = power.T[:1]
            powers = jnp.concatenate([powers, jnp.zeros((1, LANES - bands), F32)], axis=1)

            def step(c, carry):
                hits = []
                for j in range(owners_once):
                    hit = (owner_ref[...] == c * owners_once + j).astype(F32).astype(BF16)
                    hits.append(digits[...] * hit)
                moved = nt(jnp.concatenate(hits, axis=0), seated[...])
                for j in range(owners_once):
                    at = 2 * bands * j
                    block = moved[at : at + bands] + moved[at + bands : at + 2 * bands]
                    label = label_ref[pl.ds(c * owners_once + j, 1)]
                    parts = [block[:, :LANES]]
                    extra = [label[:, :LANES]]
                    if tail:
                        over = block[:, LANES:]
                        parts.append(
                            jnp.concatenate([over[: bands // 2], over[bands // 2 :]], axis=1)
                        )
                        over = label[:, LANES:]
                        extra.append(jnp.concatenate([over, over], axis=1))
                    else:
                        extra.append(jnp.zeros((1, LANES), F32))
                    extra.append(powers)
                    extra.append(jnp.zeros((5, LANES), F32))
                    out = jnp.concatenate(parts + [jnp.concatenate(extra, axis=0)], axis=0)
                    send_ref[c * owners_once + j] = out.astype(I32).astype(jnp.int16)
                return carry

            lax.fori_loop(0, devices // owners_once, step, 0)

    sources_once = 32
    tops = surfaces // LANES
    lot = sources_once * LANES * (2 if tail else 1)
    top_rows = 2 * bands + 16

    def reduce_rows(got_ref, out_ref, scales, total):
        power = got_ref[:, value_rows + 2].astype(F32)
        scale = jnp.exp2(power).T[:bands]
        for s in range(devices):
            scales[s] = jnp.broadcast_to(scale[:, s : s + 1], (bands, LANES))
        total[...] = jnp.zeros_like(total)
        left = iota((bands // 2, LANES), 1) < LANES // 2
        first_half = iota((1, LANES), 1) < LANES // 2

        def step(c, carry):
            values, labels, once_each = [], [], []
            for j in range(sources_once):
                source = c * sources_once + j
                got = got_ref[source].astype(F32)
                grown = scales[source]
                values.append(got[:bands] * grown)
                labels.append(got[value_rows : value_rows + 1])
                once_each.append(jnp.ones((1, LANES), F32))
                if tail:
                    over = got[bands:value_rows]
                    low = jnp.where(left, over * grown[: bands // 2], 0.0)
                    high = jnp.where(left, 0.0, over * grown[bands // 2 :])
                    values.append(jnp.concatenate([low, high], axis=0))
                    labels.append(got[value_rows + 1 : value_rows + 2])
                    once_each.append(jnp.where(first_half, 1.0, 0.0))
            value = jnp.concatenate(values, axis=1)
            label = jnp.concatenate(labels, axis=1).astype(I32)
            counted = jnp.concatenate(once_each, axis=1)
            high = value.astype(BF16)
            low = (value - high.astype(F32)).astype(BF16)
            counted = jnp.broadcast_to(counted, (16, lot)).astype(BF16)
            both = jnp.concatenate([high, low, counted], axis=0)
            seated = (iota((LANES, lot), 0) == (label & 127)).astype(F32).astype(BF16)
            chosen = [both * (label >> 7 == t).astype(F32).astype(BF16) for t in range(tops)]
            total[...] += nt(jnp.concatenate(chosen, axis=0), seated)
            return carry

        lax.fori_loop(0, devices // sources_once, step, 0)
        for t in range(tops):
            at = t * top_rows
            sums = total[at : at + bands] + total[at + bands : at + 2 * bands]
            count = jnp.maximum(total[at + 2 * bands : at + 2 * bands + 1], 1.0)
            out_ref[:, t * LANES : (t + 1) * LANES] = sums / count

    start = jnp.stack(lax.optimization_barrier((start, outer(start), rank, pieces))[:2])
    slots, rank, labels, _ = lax.optimization_barrier((slots, rank, labels, start))
    full, matrix, *parts = kernel_call(
        adjoint_first,
        4,
        1,
        [pl.BlockSpec(memory_space=pl.ANY)] + [along((3, part_bands, once * width), 2)] * split,
        [
            (full_rows, shape((3,) + block_shape, F32)),
            (VMEM, pltpu.VMEM(matrix.shape, BF16)),
        ]
        + part_outs,
        (slots, matrix) + tuple(pieces),
        total_scratch + [pltpu.SemaphoreType.DMA((rb_count,))],
        limit=24 * MIB,
        flops=pass_flops,
    )
    starts = gather(start, parts[0])
    got_one = collect(*parts)

    zero, rad = kernel_call(
        forward_first,
        4,
        1,
        [VMEM] + [whole((2,) + start_shape)] * split
        + [whole((split,) + start_shape), full_rows],
        [(step_rows, shape(block_shape, F32)), (step_rows, shape(block_shape, BF16))],
        (slots, matrix) + tuple(starts) + (full,),
        window_scratch,
        flops=pass_flops,
    )
    rad = pair_of(rad)
    got_one[0], _ = lax.optimization_barrier((got_one[0], rad))
    rad, _ = lax.optimization_barrier((rad, got_one))

    adjoint_one, *parts = kernel_call(
        adjoint_second,
        4,
        1,
        [VMEM] + [step_rows] * split + [full_rows],
        [(step_rows, shape(block_shape, F32))] + part_outs,
        (slots, matrix) + tuple(got_one) + (full,),
        total_scratch,
        flops=pass_flops,
    )
    rads = gather(rad, parts[0])
    got_zero = collect(*parts)

    one, radiosity = kernel_call(
        forward_second,
        4,
        1,
        [VMEM] + [whole((2,) + block_shape)] * split + [whole(part_shape), full_rows],
        [
            (step_rows, shape(block_shape, F32)),
            (along((bands, once * width), 1), shape((bands, rows), F32)),
        ],
        (slots, matrix) + tuple(rads) + (full,),
        window_scratch,
        flops=pass_flops,
    )

    (send,) = kernel_call(
        pack_rows,
        4,
        0,
        [step_rows] * (split + 3)
        + [full_rows, whole((1, rows)), whole((1, rows)), whole((devices, seats))],
        [
            (
                whole((devices, send_rows, LANES)),
                shape((devices, send_rows, LANES), jnp.int16),
            )
        ],
        (
            *got_zero,
            adjoint_one,
            zero,
            one,
            full,
            patch_owner.reshape(1, rows),
            rank,
            labels,
        ),
        [
            pltpu.VMEM((bands, rows), F32),
            pltpu.VMEM((2 * bands, rows), BF16),
            pltpu.VMEM((seats, rows), BF16),
            pltpu.VMEM((bands, LANES), F32),
        ],
    )
    send = lax.all_to_all(send, ("band", "patch"), 0, 0, tiled=True)
    (surface_grad,) = kernel_call(
        reduce_rows,
        1,
        0,
        [whole((devices, send_rows, LANES))],
        [(whole((bands, surfaces)), shape((bands, surfaces), F32))],
        (send,),
        [
            pltpu.VMEM((devices, bands, LANES), F32),
            pltpu.VMEM((tops * top_rows, LANES), F32),
        ],
    )
    return (radiosity.reshape(bands, 1, 1, rows), surface_grad)


def solution(mesh):
    in_specs = (
        P("band", "patch"),
        P("band", "patch"),
        P("band", "patch"),
        P("patch", "band", None, None, None, None),
        P("patch", "band", None, None),
        P("patch", "band", None, None),
        P("patch", "band", None),
    )
    out_specs = (P(None, "patch", "band", None), P(None, ("band", "patch")))
    return jax.shard_map(body, mesh=mesh, in_specs=in_specs, out_specs=out_specs, check_vma=False)
```

```python
import jax
import jax.numpy as jnp
from jax import lax
from jax.experimental import pallas as pl
from jax.experimental.pallas import tpu as pltpu
from jax.sharding import PartitionSpec as P

F32 = jnp.float32
BF16 = jnp.bfloat16
I32 = jnp.int32
LANES = 128
MIB = 1 << 20
VMEM = pl.BlockSpec(memory_space=pltpu.VMEM)
TOP = 32767.0
RANGES = ((0.099, 0.901), (0.199, 2.001), (0.499, 1.501))


def coded(value, a):
    low, high = RANGES[a]
    scaled = (value - low) * (65535.0 / (high - low)) - 32768.0
    return jnp.round(jnp.clip(scaled, -32768.0, 32767.0)).astype(jnp.int32).astype(jnp.int16)


def decoded(code, a):
    low, high = RANGES[a]
    return (code.astype(F32) + 32768.0) * ((high - low) / 65535.0) + low


def shape(dims, dtype):
    return jax.ShapeDtypeStruct(dims, dtype)


def whole(dims):
    return pl.BlockSpec(dims, lambda i, *_: (0,) * len(dims))


def along(dims, axis):
    return pl.BlockSpec(dims, lambda i, *_: tuple(i if d == axis else 0 for d in range(len(dims))))


def nt(a, b):
    return lax.dot_general(a, b, (((1,), (1,)), ((), ())), preferred_element_type=F32)


def nn(a, b):
    return lax.dot_general(a, b, (((1,), (0,)), ((), ())), preferred_element_type=F32)


def iota(dims, axis):
    return lax.broadcasted_iota(I32, dims, axis)


def kernel_call(kernel, steps, scalars, ins, outs, args, scratch=(), limit=24 * MIB, flops=0):
    return pl.pallas_call(
        kernel,
        out_shape=[o for _, o in outs],
        grid_spec=pltpu.PrefetchScalarGridSpec(
            num_scalar_prefetch=scalars,
            grid=(steps,),
            in_specs=ins,
            out_specs=[s for s, _ in outs],
            scratch_shapes=scratch,
        ),
        compiler_params=pltpu.CompilerParams(vmem_limit_bytes=limit),
        cost_estimate=pl.CostEstimate(flops=flops, bytes_accessed=flops // 32, transcendentals=0),
    )(*args)


def body(
    emissivity, blackbody, loss_weights, view_blocks, column_blocks, patch_owner, patch_surface
):
    split = lax.axis_size("band")
    groups = lax.axis_size("patch")
    devices = split * groups
    part_bands = emissivity.shape[0]
    bands = part_bands * split
    rb_count, depth, width = view_blocks.shape[2:5]
    rows = rb_count * width
    per_group = split * rb_count
    group_bits = per_group.bit_length() - 1
    assert 1 << group_bits == per_group
    capacity = max(2, 3 * rows // devices)
    surfaces = rows // 2

    def inner(block):
        return lax.ppermute(block, "patch", [(i, i ^ 1) for i in range(groups)])

    def outer(block):
        return lax.ppermute(
            block, "patch", [(i, (i + (1 if i % 2 else -1)) % groups) for i in range(groups)]
        )

    def across(block, d):
        return lax.ppermute(block, "band", [(i, i ^ d) for i in range(split)])

    matrix = view_blocks.reshape(rb_count, depth, width, width)
    block_shape = (rb_count, bands, width)
    part_shape = (split,) + block_shape
    pass_flops = 2 * bands * rb_count * depth * width * width
    once = rb_count // 2

    def prepare(e_hbm, b_hbm, w_hbm, start_ref, *refs):
        piece_refs, (e_ref, b_ref, w_ref, loaded) = refs[:split], refs[split:]
        band = lax.axis_index("band")
        loads = [
            pltpu.make_async_copy(source, target, loaded.at[a])
            for a, (source, target) in enumerate(((e_hbm, e_ref), (b_hbm, b_ref), (w_hbm, w_ref)))
        ]
        for load in loads:
            load.start()
        for load in loads:
            load.wait()
        for c in range(per_group):
            cut = slice(c * width, (c + 1) * width)
            start_ref[c] = (e_ref[:, cut] * b_ref[:, cut]).astype(BF16)
        for d in range(split):
            cut = pl.ds(pl.multiple_of((band ^ d) * rows, rows), rows)
            for a, ref in enumerate((e_ref, b_ref, w_ref)):
                piece_refs[d][a] = coded(ref[:, cut], a)

    piece = (3, part_bands, rows)
    start_shape = (per_group, part_bands, width)
    start, *pieces = kernel_call(
        prepare,
        1,
        0,
        [pl.BlockSpec(memory_space=pltpu.HBM)] * 3,
        [(whole(start_shape), shape(start_shape, BF16))]
        + [(whole(piece), shape(piece, jnp.int16))] * split,
        (emissivity, blackbody, loss_weights),
        [pltpu.VMEM(emissivity.shape, F32)] * 3 + [pltpu.SemaphoreType.DMA((3,))],
        limit=60 * MIB,
    )
    pieces = [across(pieces[d], d) if d else pieces[d] for d in range(split)]

    def pair_of(block):
        return jnp.stack([block, outer(block)])

    def gather(pair, after):
        pairs = [pair] + [across(pair, d) for d in range(1, split)]
        pairs, _ = lax.optimization_barrier((pairs, after))
        return pairs + [inner(jnp.stack([p[0] for p in pairs]))]

    def scatter_products(slots_ref, m_ref, value_of, outs, total):
        i = pl.program_id(0)

        @pl.when(i == 0)
        def _():
            total[...] = jnp.zeros_like(total)

        for q in range(once):
            u = value_of(q)
            for k in range(depth):
                s = slots_ref[i * once + q, k]
                total[s] += nn(u, m_ref[i * once + q, k])

        @pl.when(i == pl.num_programs(0) - 1)
        def _():
            own_ref, near_ref, far_ref = outs
            band = lax.axis_index("band")
            for d in range(split):
                at = (band ^ d) * rb_count
                own_ref[d] = total[pl.ds(at, rb_count)]
                near_ref[d] = total[pl.ds(per_group + at, rb_count)].astype(BF16)
                far_ref[d] = total[pl.ds(2 * per_group + at, rb_count)].astype(BF16)

    part_outs = [(whole(part_shape), shape(part_shape, t)) for t in (F32, BF16, BF16)]
    total_scratch = [pltpu.VMEM((3 * per_group, bands, width), F32)]
    step_rows = along((once, bands, width), 0)
    full_rows = along((3, once, bands, width), 1)

    def adjoint_first(slots_ref, matrix_ref, *refs):
        piece_refs, (full_ref, m_ref), outs = refs[:split], refs[split : split + 2], refs[split + 2 : -2]
        total, arrivals = refs[-2:]
        i = pl.program_id(0)

        def copy_of(r):
            return pltpu.make_async_copy(matrix_ref.at[r], m_ref.at[r], arrivals.at[r])

        @pl.when(i == 0)
        def _():
            for r in range(rb_count):
                copy_of(r).start()

        b = lax.axis_index("band")
        for d in range(split):
            at = pl.ds(pl.multiple_of((b ^ d) * part_bands, part_bands), part_bands)
            for a in range(3):
                for q in range(once):
                    code = piece_refs[d][a, :, q * width : (q + 1) * width]
                    full_ref[a, q, at, :] = decoded(code, a)

        def value_of(q):
            copy_of(i * once + q).wait()
            return ((1.0 - full_ref[0, q]) * full_ref[2, q]).astype(BF16)

        scatter_products(slots_ref, m_ref, value_of, outs, total)

    def arrived(refs, q):
        value = refs[0][q]
        for ref in refs[1:]:
            value = value + ref[q].astype(F32)
        return value

    def adjoint_second(slots_ref, m_ref, *refs):
        got_refs, (full_ref, one_ref), outs, total = (
            refs[:split],
            refs[split : split + 2],
            refs[split + 2 : -1],
            refs[-1],
        )

        def value_of(q):
            value = arrived(got_refs, q)
            one_ref[q] = value
            return ((1.0 - full_ref[0, q]) * value).astype(BF16)

        scatter_products(slots_ref, m_ref, value_of, outs, total)

    def merge(own_ref, near_ref, far_ref, kept_ref, *sent_refs):
        for d in range(split):
            value = own_ref[d] + near_ref[d].astype(F32) + far_ref[d].astype(F32)
            if d:
                sent_refs[d - 1][...] = value.astype(BF16)
            else:
                kept_ref[...] = value

    def collect(own, near, far):
        kept, *sent = kernel_call(
            merge,
            1,
            0,
            [whole(part_shape)] * 3,
            [(whole(block_shape), shape(block_shape, F32))]
            + [(whole(block_shape), shape(block_shape, BF16))] * (split - 1),
            (own, inner(near), outer(far)),
        )
        return [kept] + [across(sent[d - 1], d) for d in range(1, split)]

    def products(slots_ref, m_ref, held, finish):
        i = pl.program_id(0)
        for q in range(once):
            value = jnp.zeros((bands, width), F32)
            for k in range(depth):
                s = slots_ref[i * once + q, k]
                value = value + nt(held[s], m_ref[i * once + q, k])
            finish(q, value)

    def forward_first(slots_ref, m_ref, *refs):
        pair_refs, (near_ref, full_ref, zero_ref, rad_ref, held) = refs[:split], refs[split:]
        band = lax.axis_index("band")

        @pl.when(pl.program_id(0) == 0)
        def _():
            def fill(c, carry):
                for third_index in range(3):
                    if third_index == 1:
                        parts = [near_ref[d, c].astype(F32) for d in range(split)]
                    else:
                        parts = [ref[third_index // 2, c].astype(F32) for ref in pair_refs]
                    held[third_index * per_group + c] = jnp.concatenate(parts, axis=0).astype(BF16)
                return carry

            lax.fori_loop(0, per_group, fill, 0)

        def finish(q, value):
            for d in range(split):
                at = pl.ds(pl.multiple_of((band ^ d) * part_bands, part_bands), part_bands)
                zero_ref[q, at, :] = value[d * part_bands : (d + 1) * part_bands]
            e, b = full_ref[0, q], full_ref[1, q]
            rad_ref[q] = (e * b + (1.0 - e) * zero_ref[q]).astype(BF16)

        products(slots_ref, m_ref, held, finish)

    def forward_second(slots_ref, m_ref, *refs):
        pair_refs, (near_ref, full_ref, one_ref, rad_ref, held) = refs[:split], refs[split:]

        @pl.when(pl.program_id(0) == 0)
        def _():
            b = lax.axis_index("band")
            for d in range(split):
                at = (b ^ d) * rb_count
                held[pl.ds(at, rb_count)] = pair_refs[d][0]
                held[pl.ds(per_group + at, rb_count)] = near_ref[d]
                held[pl.ds(2 * per_group + at, rb_count)] = pair_refs[d][1]

        def finish(q, value):
            one_ref[q] = value
            e, b = full_ref[0, q], full_ref[1, q]
            rad_ref[:, q * width : (q + 1) * width] = e * b + (1.0 - e) * value

        products(slots_ref, m_ref, held, finish)

    window_scratch = [pltpu.VMEM((3 * per_group, bands, width), BF16)]

    tail = max(0, capacity - LANES)
    seats = LANES + (LANES // 2 if tail else 0)
    value_rows = bands + (bands // 2 if tail else 0)
    send_rows = value_rows + 8

    def route(column_ref, owner_ref, surface_ref, slot_ref, rank_ref, label_ref):
        me = lax.axis_index("patch")
        column = column_ref[...]
        group = jnp.right_shift(column, group_bits)
        third = jnp.where(group == me, 0, jnp.where(group == (me ^ 1), 1, 2))
        slot_ref[...] = third * per_group + jnp.bitwise_and(column, per_group - 1)
        names = iota((devices, width), 0)
        upper = (iota((width, width), 0) <= iota((width, width), 1)).astype(BF16)
        seat = iota((seats, width), 0)
        count = jnp.zeros((devices, 1), F32)
        found = jnp.zeros((3 * devices, seats), F32)
        for c in range(rb_count):
            cut = slice(c * width, (c + 1) * width)
            hit = (owner_ref[:, cut] == names).astype(F32)
            rank = nn(hit.astype(BF16), upper) + count
            count = rank[:, width - 1 : width]
            place = jnp.sum(hit * rank, axis=0, keepdims=True).astype(I32) - 1
            rank_ref[:, cut] = place
            seated = (seat == place).astype(F32).astype(BF16)
            surface = surface_ref[:, cut]
            high = (surface >> 7).astype(F32)
            low = (surface & 127).astype(F32)
            marks = jnp.concatenate([hit, hit * high, hit * low], axis=0).astype(BF16)
            found = found + nt(marks, seated)
        taken, high, low = (found[a * devices : (a + 1) * devices] for a in range(3))
        label_ref[...] = jnp.where(taken > 0.5, high * 128.0 + low, float(surfaces))

    slots, rank, labels = kernel_call(
        route,
        1,
        0,
        [whole((rb_count, depth))] + [whole((1, rows))] * 2,
        [
            (whole((rb_count, depth)), shape((rb_count, depth), I32)),
            (whole((1, rows)), shape((1, rows), I32)),
            (whole((devices, seats)), shape((devices, seats), F32)),
        ],
        (
            column_blocks.reshape(rb_count, depth),
            patch_owner.reshape(1, rows),
            patch_surface.reshape(1, rows),
        ),
        limit=60 * MIB,
    )

    owners_once = 32

    def pack_rows(*refs):
        got_refs = refs[:split]
        adj_ref, zero_ref, one_ref, full_ref, owner_ref, rank_ref, label_ref = refs[
            split : split + 7
        ]
        send_ref, grad, digits, seated, most = refs[split + 7 :]
        i = pl.program_id(0)

        @pl.when(i == 0)
        def _():
            most[...] = jnp.full_like(most, 1e-30)

        for q in range(once):
            b, w = full_ref[1, q], full_ref[2, q]
            a = adj_ref[q]
            value = (w + a + arrived(got_refs, q)) * b - (w * one_ref[q] + a * zero_ref[q])
            cut = pl.ds(pl.multiple_of((i * once + q) * width, width), width)
            grad[:, cut] = value
            most[...] = jnp.maximum(most[...], jnp.max(jnp.abs(value), axis=1, keepdims=True))

        @pl.when(i == pl.num_programs(0) - 1)
        def _():
            power = jnp.floor(jnp.log2(most[...])) - 14.0
            power = jnp.where(most[...] * jnp.exp2(-power) > TOP, power + 1.0, power)
            scale = jnp.exp2(-power)[:, :1]
            ordinal = jnp.round(jnp.clip(grad[...] * scale, -TOP, TOP))
            high = ordinal.astype(BF16)
            digits[:bands] = high
            digits[bands:] = (ordinal - high.astype(F32)).astype(BF16)
            seated[...] = (iota((seats, rows), 0) == rank_ref[...]).astype(F32).astype(BF16)
            powers = power.T[:1]
            powers = jnp.concatenate([powers, jnp.zeros((1, LANES - bands), F32)], axis=1)

            def step(c, carry):
                hits = []
                for j in range(owners_once):
                    hit = (owner_ref[...] == c * owners_once + j).astype(F32).astype(BF16)
                    hits.append(digits[...] * hit)
                moved = nt(jnp.concatenate(hits, axis=0), seated[...])
                for j in range(owners_once):
                    at = 2 * bands * j
                    block = moved[at : at + bands] + moved[at + bands : at + 2 * bands]
                    label = label_ref[pl.ds(c * owners_once + j, 1)]
                    parts = [block[:, :LANES]]
                    extra = [label[:, :LANES]]
                    if tail:
                        over = block[:, LANES:]
                        parts.append(
                            jnp.concatenate([over[: bands // 2], over[bands // 2 :]], axis=1)
                        )
                        over = label[:, LANES:]
                        extra.append(jnp.concatenate([over, over], axis=1))
                    else:
                        extra.append(jnp.zeros((1, LANES), F32))
                    extra.append(powers)
                    extra.append(jnp.zeros((5, LANES), F32))
                    out = jnp.concatenate(parts + [jnp.concatenate(extra, axis=0)], axis=0)
                    send_ref[c * owners_once + j] = out.astype(I32).astype(jnp.int16)
                return carry

            lax.fori_loop(0, devices // owners_once, step, 0)

    sources_once = 32
    tops = surfaces // LANES
    lot = sources_once * LANES * (2 if tail else 1)
    top_rows = 2 * bands + 16

    def reduce_rows(got_ref, out_ref, scales, total):
        power = got_ref[:, value_rows + 2].astype(F32)
        scale = jnp.exp2(power).T[:bands]
        for s in range(devices):
            scales[s] = jnp.broadcast_to(scale[:, s : s + 1], (bands, LANES))
        total[...] = jnp.zeros_like(total)
        left = iota((bands // 2, LANES), 1) < LANES // 2
        first_half = iota((1, LANES), 1) < LANES // 2

        def step(c, carry):
            values, labels, once_each = [], [], []
            for j in range(sources_once):
                source = c * sources_once + j
                got = got_ref[source].astype(F32)
                grown = scales[source]
                values.append(got[:bands] * grown)
                labels.append(got[value_rows : value_rows + 1])
                once_each.append(jnp.ones((1, LANES), F32))
                if tail:
                    over = got[bands:value_rows]
                    low = jnp.where(left, over * grown[: bands // 2], 0.0)
                    high = jnp.where(left, 0.0, over * grown[bands // 2 :])
                    values.append(jnp.concatenate([low, high], axis=0))
                    labels.append(got[value_rows + 1 : value_rows + 2])
                    once_each.append(jnp.where(first_half, 1.0, 0.0))
            value = jnp.concatenate(values, axis=1)
            label = jnp.concatenate(labels, axis=1).astype(I32)
            counted = jnp.concatenate(once_each, axis=1)
            high = value.astype(BF16)
            low = (value - high.astype(F32)).astype(BF16)
            counted = jnp.broadcast_to(counted, (16, lot)).astype(BF16)
            both = jnp.concatenate([high, low, counted], axis=0)
            seated = (iota((LANES, lot), 0) == (label & 127)).astype(F32).astype(BF16)
            chosen = [both * (label >> 7 == t).astype(F32).astype(BF16) for t in range(tops)]
            total[...] += nt(jnp.concatenate(chosen, axis=0), seated)
            return carry

        lax.fori_loop(0, devices // sources_once, step, 0)
        for t in range(tops):
            at = t * top_rows
            sums = total[at : at + bands] + total[at + bands : at + 2 * bands]
            count = jnp.maximum(total[at + 2 * bands : at + 2 * bands + 1], 1.0)
            out_ref[:, t * LANES : (t + 1) * LANES] = sums / count

    start = jnp.stack(lax.optimization_barrier((start, outer(start), rank, pieces))[:2])
    slots, rank, labels, _ = lax.optimization_barrier((slots, rank, labels, start))
    full, matrix, *parts = kernel_call(
        adjoint_first,
        2,
        1,
        [pl.BlockSpec(memory_space=pl.ANY)] + [along((3, part_bands, once * width), 2)] * split,
        [
            (full_rows, shape((3,) + block_shape, F32)),
            (VMEM, pltpu.VMEM(matrix.shape, BF16)),
        ]
        + part_outs,
        (slots, matrix) + tuple(pieces),
        total_scratch + [pltpu.SemaphoreType.DMA((rb_count,))],
        limit=24 * MIB,
        flops=pass_flops,
    )
    starts = gather(start, parts[0])
    got_one = collect(*parts)

    zero, rad = kernel_call(
        forward_first,
        2,
        1,
        [VMEM] + [whole((2,) + start_shape)] * split
        + [whole((split,) + start_shape), full_rows],
        [(step_rows, shape(block_shape, F32)), (step_rows, shape(block_shape, BF16))],
        (slots, matrix) + tuple(starts) + (full,),
        window_scratch,
        flops=pass_flops,
    )
    rad = pair_of(rad)
    got_one[0], _ = lax.optimization_barrier((got_one[0], rad))
    rad, _ = lax.optimization_barrier((rad, got_one))

    adjoint_one, *parts = kernel_call(
        adjoint_second,
        2,
        1,
        [VMEM] + [step_rows] * split + [full_rows],
        [(step_rows, shape(block_shape, F32))] + part_outs,
        (slots, matrix) + tuple(got_one) + (full,),
        total_scratch,
        flops=pass_flops,
    )
    rads = gather(rad, parts[0])
    got_zero = collect(*parts)

    one, radiosity = kernel_call(
        forward_second,
        2,
        1,
        [VMEM] + [whole((2,) + block_shape)] * split + [whole(part_shape), full_rows],
        [
            (step_rows, shape(block_shape, F32)),
            (along((bands, once * width), 1), shape((bands, rows), F32)),
        ],
        (slots, matrix) + tuple(rads) + (full,),
        window_scratch,
        flops=pass_flops,
    )

    (send,) = kernel_call(
        pack_rows,
        2,
        0,
        [step_rows] * (split + 3)
        + [full_rows, whole((1, rows)), whole((1, rows)), whole((devices, seats))],
        [
            (
                whole((devices, send_rows, LANES)),
                shape((devices, send_rows, LANES), jnp.int16),
            )
        ],
        (
            *got_zero,
            adjoint_one,
            zero,
            one,
            full,
            patch_owner.reshape(1, rows),
            rank,
            labels,
        ),
        [
            pltpu.VMEM((bands, rows), F32),
            pltpu.VMEM((2 * bands, rows), BF16),
            pltpu.VMEM((seats, rows), BF16),
            pltpu.VMEM((bands, LANES), F32),
        ],
    )
    send = lax.all_to_all(send, ("band", "patch"), 0, 0, tiled=True)
    (surface_grad,) = kernel_call(
        reduce_rows,
        1,
        0,
        [whole((devices, send_rows, LANES))],
        [(whole((bands, surfaces)), shape((bands, surfaces), F32))],
        (send,),
        [
            pltpu.VMEM((devices, bands, LANES), F32),
            pltpu.VMEM((tops * top_rows, LANES), F32),
        ],
    )
    return (radiosity.reshape(bands, 1, 1, rows), surface_grad)


def solution(mesh):
    in_specs = (
        P("band", "patch"),
        P("band", "patch"),
        P("band", "patch"),
        P("patch", "band", None, None, None, None),
        P("patch", "band", None, None),
        P("patch", "band", None, None),
        P("patch", "band", None),
    )
    out_specs = (P(None, "patch", "band", None), P(None, ("band", "patch")))
    return jax.shard_map(body, mesh=mesh, in_specs=in_specs, out_specs=out_specs, check_vma=False)
```
